32 devices in a mesh: leaf: 8 (over z, x), task: 4 (over y, core).
Axes of the slice: x: 2, y: 2, z: 4, core: 2. Of those that a mesh axis runs over, the one named last changes fastest.
Arguments:
- points: bfloat16 [131072, 64], P(('leaf', 'task')), may hold values from -6 to 6
- weights: bfloat16 [131072, 64], P(('leaf', 'task')), may hold values from -4 to 4
- point_order: int32 [8, 4, 4096], P('leaf', 'task'), may hold values from 0 to 4095, each once within a row
- node_order: int32 [8, 4, 4096], P('leaf', 'task'), may hold values from 0 to 4095, each once within a row
- merge_order: int32 [8, 4, 2, 1024], P('leaf', 'task'), may hold values from 0 to 1023, as said below
- far_list: int32 [8, 4, 4, 3], P('leaf', 'task'), may hold values 0 or 1
- task_target: int32 [8, 4, 4, 1], P('leaf', 'task'), may hold values from -1 to 3, as said below
- task_source: int32 [8, 4, 4, 1], P('leaf', 'task'), may hold values from 0 to 3
Outputs:
- potentials: float32 [131072, 64], P(('leaf', 'task'))
The draws below stay inside these ranges and needn't reach their ends.
Inputs may be any that keep to these rules, and one draw needn't show every extreme that they name: `merge_order`: each row is a permutation of 0 to 1023; rows [i, j, b] are equal for all i with the same i // 2 ** (b + 1). `task_target`: -1 marks an empty slot; every device of every draw has a slab toward which all 1 slots are used.
All inputs are finite; a program needn't handle non-finite values. No bound on the sum of `far_list` on one device may be relied on, other than what follows from the above.
Results may differ from the reference program's by a relative error of at most 0.002.
Values may be sent and summed in bfloat16 or wider, within the bound.
A program may use at most 64 MiB of HBM per device.

```python
import jax
import jax.numpy as jnp
from jax import lax

F = 64
C = 64
LEAF_PTS = 1024
SKEL = 512
LEVELS = 3
LEAF_DEV = 4
CAP = 1
PTS_DEV = 4096
MERGES = 2
REGIONS = 8
SLABS = 4
POINTS = 131072


def draw_merge_order(key, part):
    base_key = jax.random.fold_in(key, 7)
    key_list = jax.random.split(base_key, REGIONS * SLABS * MERGES)
    shuffles = jax.vmap(lambda one_key: jax.random.permutation(one_key, 2 * SKEL))(key_list)
    shuffles = shuffles.reshape(REGIONS, SLABS, MERGES, 2 * SKEL)
    per_tier = []
    for tier_index in range(MERGES):
        stride_len = 2 ** (tier_index + 1)
        leaders = jnp.arange(REGIONS) // stride_len * stride_len
        per_tier.append(shuffles[leaders, :, tier_index, :])
    return jnp.stack(per_tier, axis=2).astype(jnp.int32)


def draw_task_target(key, part):
    busy_key, roll_key, leaf_key = jax.random.split(jax.random.fold_in(key, 11), 3)
    busyness = jax.random.randint(busy_key, (REGIONS, 1, SLABS, 1), 1, 5)
    rolled = jax.random.randint(roll_key, (REGIONS, SLABS, SLABS, CAP), 0, 4)
    chosen = jax.random.randint(leaf_key, (REGIONS, SLABS, SLABS, CAP), 0, LEAF_DEV)
    sender = jnp.arange(SLABS)[None, :, None, None]
    receiver = jnp.arange(SLABS)[None, None, :, None]
    forced = receiver == (sender + 1) % SLABS
    return jnp.where((rolled < busyness) | forced, chosen, -1).astype(jnp.int32)


def with_ends(array, rng, smallest, top_value):
    index_at = [jax.random.randint(jax.random.fold_in(rng, axis), (), 0, length) for axis, length in enumerate(array.shape)]
    main_axis = array.shape.index(max(array.shape))
    neighbour = index_at[:main_axis] + [(index_at[main_axis] + 1) % array.shape[main_axis]] + index_at[main_axis + 1:]
    return array.at[tuple(index_at)].set(smallest).at[tuple(neighbour)].set(top_value)


def steps_of(own_key, shape, cuts, low, top_value):
    def one(position, parts):
        draws = jax.random.uniform(jax.random.fold_in(jax.random.fold_in(own_key, 6), position), (parts,), jnp.float32, low / len(cuts), top_value / len(cuts))
        return jnp.repeat(jnp.exp(draws), shape[position] // parts).reshape((-1,) + (1,) * (len(shape) - position - 1))

    factor_of = one(*cuts[0])
    for cut in cuts[1:]:
        factor_of = factor_of * one(*cut)
    return factor_of


def noise(stream_key, extent, width, most, cuts=(), held_as=jnp.bfloat16):
    values = jax.random.normal(stream_key, extent, jnp.float32) * width
    if len(cuts) > 0:
        values = steps_of(stream_key, extent, cuts, -0.22, 0.18) * values
    return jnp.clip(values, min=-most, max=most).astype(held_as)


def setup_inputs(seed: int = 0) -> dict:
    key_of = jax.random.split(jax.random.key(seed), 9)
    return {
        "points": noise(key_of[0], (POINTS, F), 1.0, 6.0, ((0, 32),)),
        "weights": noise(key_of[1], (POINTS, C), 0.5, 4.0, ((0, 32),)),
        "point_order": jax.vmap(lambda own: jax.random.permutation(own, PTS_DEV))(jax.random.split(key_of[2], REGIONS * SLABS)).reshape((REGIONS, SLABS, PTS_DEV)).astype(jnp.int32),
        "node_order": jax.vmap(lambda own: jax.random.permutation(own, PTS_DEV))(jax.random.split(key_of[3], REGIONS * SLABS)).reshape((REGIONS, SLABS, PTS_DEV)).astype(jnp.int32),
        "merge_order": draw_merge_order(jax.random.fold_in(key_of[8], 71), 0),
        "far_list": with_ends((jax.random.randint(key_of[5], (REGIONS, SLABS, LEAF_DEV, LEVELS), 0, 4) < 3).astype(jnp.int32), jax.random.fold_in(key_of[5], 1), 0, 1),
        "task_target": draw_task_target(jax.random.fold_in(key_of[8], 71), 0),
        "task_source": with_ends(jax.random.randint(key_of[7], (REGIONS, SLABS, SLABS, CAP), 0, LEAF_DEV), jax.random.fold_in(key_of[7], 1), 0, LEAF_DEV - 1).astype(jnp.int32),
    }


KERNEL_SCALE = 1.5


def kernel(left_pts, right_pts):
    cross_term = jnp.dot(left_pts, right_pts.T, preferred_element_type=jnp.float32)
    left_norm = jnp.sum(jnp.square(left_pts.astype(jnp.float32)), axis=1)
    right_norm = jnp.sum(jnp.square(right_pts.astype(jnp.float32)), axis=1)
    distance = left_norm[:, None] + right_norm[None, :] - 2.0 * cross_term
    return jnp.exp((-KERNEL_SCALE / left_pts.shape[1]) * distance)


def anterpolate(skel_x, rest_x, skel_w, rest_w):
    dense = kernel(skel_x, rest_x)
    spread = (dense / jnp.sum(dense, axis=0, keepdims=True)).astype(jnp.bfloat16)
    summed = skel_w.astype(jnp.float32) + jnp.dot(spread, rest_w, preferred_element_type=jnp.float32)
    return summed.astype(jnp.bfloat16)


def merge_node(payload):
    picked_x, picked_w = payload
    return picked_x[:SKEL], anterpolate(picked_x[:SKEL], picked_x[SKEL:], picked_w[:SKEL], picked_w[SKEL:])


def level_zero(payload):
    tree_x, tree_w, node_pick = payload
    return merge_node((tree_x[node_pick], tree_w[node_pick]))


def reference(points, weights, point_order, node_order, merge_order, far_list, task_target, task_source):
    features = points.shape[1]
    columns = weights.shape[1]
    devices = REGIONS * SLABS
    block_x = points.reshape(devices, PTS_DEV, features)
    block_w = weights.reshape(devices, PTS_DEV, columns)
    tree_order = point_order.reshape(devices, PTS_DEV)
    tree_x = jax.vmap(lambda rows_x, picks: rows_x[picks])(block_x, tree_order)
    tree_w = jax.vmap(lambda rows_w, picks: rows_w[picks])(block_w, tree_order)
    node_x, node_w = lax.map(level_zero, (tree_x, tree_w, node_order.reshape(devices, PTS_DEV)))
    node_x = node_x.reshape(REGIONS, SLABS, SKEL, features)
    node_w = node_w.reshape(REGIONS, SLABS, SKEL, columns)
    region = jnp.arange(REGIONS)
    sibling_x = []
    sibling_w = []
    for level_index in range(LEVELS):
        partner = region ^ (1 << level_index)
        other_x = node_x[partner]
        other_w = node_w[partner]
        sibling_x.append(other_x)
        sibling_w.append(other_w)
        if level_index < LEVELS - 1:
            upper = (((region >> level_index) & 1) == 1)[:, None, None, None]
            cat_x = jnp.concatenate([jnp.where(upper, other_x, node_x), jnp.where(upper, node_x, other_x)], axis=2)
            cat_w = jnp.concatenate([jnp.where(upper, other_w, node_w), jnp.where(upper, node_w, other_w)], axis=2)
            merge_rows = merge_order[:, :, level_index, :]
            picked_x = jnp.take_along_axis(cat_x, merge_rows[..., None], axis=2)
            picked_w = jnp.take_along_axis(cat_w, merge_rows[..., None], axis=2)
            new_x, new_w = lax.map(merge_node, (picked_x.reshape(devices, 2 * SKEL, features), picked_w.reshape(devices, 2 * SKEL, columns)))
            node_x = new_x.reshape(REGIONS, SLABS, SKEL, features)
            node_w = new_w.reshape(REGIONS, SLABS, SKEL, columns)
    stack_x = jnp.stack(sibling_x, axis=2).reshape(devices, LEVELS, SKEL, features)
    stack_w = jnp.stack(sibling_w, axis=2).reshape(devices, LEVELS, SKEL, columns)
    leaves_x = tree_x.reshape(REGIONS, SLABS, LEAF_DEV, LEAF_PTS, features)
    leaves_w = tree_w.reshape(REGIONS, SLABS, LEAF_DEV, LEAF_PTS, columns)
    far_flags = far_list.reshape(devices, LEAF_DEV, LEVELS)
    targets_all = task_target.reshape(devices, SLABS, CAP)
    sources_all = task_source.reshape(devices, SLABS, CAP)

    def pair_terms(payload):
        target_x, source_x, source_w = payload

        def single(one_t, one_s, one_w):
            return jnp.dot(kernel(one_t, one_s).astype(jnp.bfloat16), one_w, preferred_element_type=jnp.float32)

        return jax.vmap(single)(target_x, source_x, source_w)

    def device_sum(device):
        region_index = device // SLABS
        slab_index = device % SLABS
        own_x = tree_x[device]
        far_field = jnp.zeros((LEAF_DEV, LEAF_PTS, columns), jnp.float32)
        for level_index in range(LEVELS):
            dense = kernel(own_x, stack_x[device, level_index]).astype(jnp.bfloat16)
            far_part = jnp.dot(dense, stack_w[device, level_index], preferred_element_type=jnp.float32)
            flags = far_flags[device, :, level_index].astype(jnp.float32)
            far_field = far_field + far_part.reshape(LEAF_DEV, LEAF_PTS, columns) * flags[:, None, None]
        target = targets_all[device]
        source = sources_all[device]
        is_live = target >= 0
        slot_leaf = jnp.maximum(target, 0)
        own_leaves = leaves_x[region_index, slab_index]
        peer_rows = jnp.arange(SLABS)[:, None]
        chosen_x = leaves_x[region_index][peer_rows, source]
        chosen_w = leaves_w[region_index][peer_rows, source]
        slot_terms = lax.map(pair_terms, (own_leaves[slot_leaf], chosen_x, chosen_w))
        onehot = ((slot_leaf[..., None] == jnp.arange(LEAF_DEV)[None, None, :]) & is_live[..., None]).astype(jnp.float32)
        near_field = jnp.einsum('pcl,pcte->lte', onehot, slot_terms, precision=lax.Precision.HIGHEST)
        return (far_field + near_field).reshape(PTS_DEV, columns)

    result = lax.map(device_sum, jnp.arange(devices))
    return result.reshape(POINTS, columns)
```

```python
import functools
import math

import jax
import jax.numpy as jnp
from jax import lax
from jax.experimental import pallas as pl
from jax.experimental.pallas import tpu as pltpu
from jax.sharding import PartitionSpec as P

SKEL = 512
KERNEL_SCALE = 1.5
LANES = 128
BF = jnp.bfloat16
F32 = jnp.float32

VMEM = pl.BlockSpec(memory_space=pltpu.VMEM)
HBM = pl.BlockSpec(memory_space=pltpu.HBM)
MESH = pl.DeviceIdType.MESH
NT = (((1,), (1,)), ((), ()))
GROUP = 64
TILE = 512


def scale_of(features):
    return KERNEL_SCALE / features * math.log2(math.e)


def bias_of(features):
    return float(int(64 / scale_of(features)) // 16 * 16)


def pieces(norm):
    first = norm.astype(BF).astype(F32)
    left = norm - first
    second = left.astype(BF).astype(F32)
    third = left - second
    return first, second, third


def columns_form(points, width, left, bias=0.0):
    features, count = points.shape
    first, second, third = pieces(jnp.sum(points * points, axis=0, keepdims=True))
    lines = lax.broadcasted_iota(jnp.int32, (8, count), 0)
    at = 0 if left else 3
    ones = 3 - at
    tail = jnp.where((lines >= ones) & (lines < ones + 3), 1.0, 0.0)
    tail = jnp.where(lines == at, -first, tail)
    tail = jnp.where(lines == at + 1, -second, tail)
    tail = jnp.where(lines == at + 2, -third, tail)
    tail = jnp.where(lines == 6, bias if left else 1.0, tail)
    rest = jnp.zeros((width - features - 8, count), F32)
    return jnp.concatenate([points + points if left else points, tail, rest], axis=0)


def dense_of(exponent, features):
    return jnp.exp2(exponent * scale_of(features))


def kept_table(index, count):
    lanes = lax.broadcasted_iota(jnp.int32, index.shape, 1)
    high = jnp.where(index // LANES == lanes, 1.0, 0.0).T.astype(BF)
    low = jnp.where(index % LANES == lanes, 1.0, 0.0).astype(BF)
    return 1.0 - jnp.dot(high, low, preferred_element_type=F32)


def kept_row(table, start, count):
    rows = [table[at : at + 1, :] for at in range(start // LANES, (start + count) // LANES)]
    return jnp.concatenate(rows, axis=1)


def pick_rows(index_of, rows_ref, skel_ref, index_ref):
    width = rows_ref.shape[1]

    def pick(step, carry):
        base = pl.multiple_of(step * GROUP, GROUP)
        found = [index_of(base + inner) for inner in range(GROUP)]
        rows = [rows_ref[index][None] for index in found]
        for inner, (index, row) in enumerate(zip(found, rows)):
            skel_ref[pl.ds(base + inner, 1), :] = row
            index_ref[pl.ds(base + inner, 1), :] = jnp.full((1, width), index, jnp.int32)
        return carry

    lax.fori_loop(0, SKEL // GROUP, pick, 0)


def run_tiles(features, tiles):
    held = None
    for exponent, use in tiles:
        value = exponent()
        if held is not None:
            held[1](dense_of(held[0], features).astype(BF))
        held = (value, use)
    held[1](dense_of(held[0], features).astype(BF))


def chain_kernel(features, levels, slabs, points_in, weights_in, order_in, node_order_in, merge_in,
                 far_in, source_in, target_in,
                 out_ref, near_out_ref, left_ref, last_right_ref, last_weight_ref,
                 points_ref, weights_ref, rows_ref, picked_ref, right_ref, skel_ref, index_ref,
                 dense_ref, part_ref, total_ref, tree_ref, pt_ref, pt_held, wt_ref, wt_held,
                 pair_pt, pair_wt, pair_rows, spread_ref, near_right_ref, far_right_ref,
                 asked_ref, send_ref, near_ref,
                 order_ref, node_order_ref, merge_ref, far_ref, target_ref, source_ref,
                 input_sem, pt_send, pt_recv, wt_send, wt_recv, ask_send, ask_recv, near_send, near_recv):
    loads = [
        pltpu.make_async_copy(source, target, input_sem.at[at])
        for at, (source, target) in enumerate([
            (points_in, points_ref),
            (weights_in, weights_ref),
            (order_in, order_ref),
            (node_order_in, node_order_ref),
            (merge_in, merge_ref),
            (far_in, far_ref),
            (source_in, source_ref),
            (target_in, target_ref),
        ])
    ]
    for load in loads:
        load.start()
    region = lax.axis_index("leaf")
    slab = lax.axis_index("task")
    count = rows_ref.shape[0]
    width = rows_ref.shape[1]
    leaves = left_ref.shape[0]
    leaf = count // leaves
    cap = source_ref.shape[0]
    chunks = count // SKEL

    def bit(level):
        return region // 2**level % 2

    def sibling(level):
        return region + (1 - 2 * bit(level)) * 2**level

    def ahead(step):
        return lax.rem(slab + step, slabs)

    def behind(step):
        return lax.rem(slab + slabs - step, slabs)

    barrier = pltpu.get_barrier_semaphore()
    for level in range(levels):
        pl.semaphore_signal(barrier, inc=1, device_id=(sibling(level), slab), device_id_type=MESH)
    for step in range(1, slabs):
        pl.semaphore_signal(barrier, inc=1, device_id=(region, ahead(step)), device_id_type=MESH)

    def to_sibling(level, source, target, send, recv):
        return pltpu.make_async_remote_copy(
            src_ref=source.at[level],
            dst_ref=target.at[level],
            send_sem=send.at[level],
            recv_sem=recv.at[level],
            device_id=(sibling(level), slab),
            device_id_type=MESH,
        )

    def pt_copy(level):
        return to_sibling(level, pt_ref, pt_held, pt_send, pt_recv)

    def wt_copy(level):
        return to_sibling(level, wt_ref, wt_held, wt_send, wt_recv)

    def ask_copy(step):
        return pltpu.make_async_remote_copy(
            src_ref=source_ref,
            dst_ref=asked_ref.at[step],
            send_sem=ask_send.at[step],
            recv_sem=ask_recv.at[step],
            device_id=(region, ahead(step)),
            device_id_type=MESH,
        )

    def near_copy(step):
        return pltpu.make_async_remote_copy(
            src_ref=send_ref.at[step],
            dst_ref=near_ref.at[step],
            send_sem=near_send.at[step],
            recv_sem=near_recv.at[step],
            device_id=(region, behind(step)),
            device_id_type=MESH,
        )

    for load in loads:
        load.wait()
    for at in range(chunks):
        part = points_ref[:, at * SKEL : (at + 1) * SKEL].astype(F32)
        both = jnp.concatenate(
            [part, weights_ref[:, at * SKEL : (at + 1) * SKEL].astype(F32)], axis=0
        )
        rows_ref[at * SKEL : (at + 1) * SKEL, :] = both.T
        right_ref[at] = columns_form(part, width, False).astype(BF)
    pick_rows(lambda at: order_ref[node_order_ref[at]], rows_ref, skel_ref, index_ref)
    skel = skel_ref[...].T
    pt_ref[0] = skel[:features].astype(BF)
    pl.semaphore_wait(barrier, levels + slabs - 1)
    pt_copy(0).start()
    for step in range(1, slabs):
        ask_copy(step).start()

    left = columns_form(skel[:features], width, True, bias_of(features)).T.astype(BF)
    table = kept_table(index_ref[...], count)
    total_ref[...] = skel[features:]

    def gather(at):
        for inner in range(SKEL):
            picked_ref[at * SKEL + inner : at * SKEL + inner + 1, :] = rows_ref[
                order_ref[at * SKEL + inner]
            ][None]

    def absorb(at):
        total_ref[...] += lax.dot_general(
            part_ref[at % 2], dense_ref[at % 2], NT, preferred_element_type=F32
        )

    for at in range(chunks):
        gather(at)
        dense = dense_of(jnp.dot(left, right_ref[at], preferred_element_type=F32), features)
        if at > 0:
            absorb(at - 1)
        share = kept_row(table, at * SKEL, SKEL) / jnp.sum(dense, axis=0, keepdims=True)
        dense_ref[at % 2] = dense.astype(BF)
        part_ref[at % 2] = (
            weights_ref[:, at * SKEL : (at + 1) * SKEL].astype(F32) * share
        ).astype(BF)
    absorb(chunks - 1)
    wt_ref[0] = total_ref[...].astype(BF)
    wt_copy(0).start()

    for one in range(leaves):
        for start in range(0, leaf, SKEL):
            turn = picked_ref[one * leaf + start : one * leaf + start + SKEL, :].T
            tree_ref[one, :, start : start + SKEL] = turn.astype(BF)
            left_ref[one, :, start : start + SKEL] = columns_form(
                turn[:features], width, True
            ).astype(BF)

    def fill(slot_ref, step, table):
        own = lax.broadcasted_iota(jnp.int32, table.shape, 1) == slab
        place = lax.broadcasted_iota(jnp.int32, table.shape, 0)
        for one in range(cap):
            wanted = jnp.max(
                jnp.where(own & (place == one), table, 0).astype(F32), axis=(0, 1), keepdims=True
            )
            for start in range(0, width, 64):
                rows = tree_ref[0, start : start + 64, :].astype(F32)
                for other in range(1, leaves):
                    rows = jnp.where(
                        wanted == other, tree_ref[other, start : start + 64, :].astype(F32), rows
                    )
                slot_ref[step, one, start : start + 64, :] = rows.astype(BF)

    for step in range(1, slabs):
        ask_copy(step).wait_recv()
        fill(send_ref, step, asked_ref[step])
        near_copy(step).start()
    fill(near_ref, 0, source_ref[...])

    def merge_points(level):
        upper = bit(level)
        pair_pt[upper] = pt_ref[level]
        pair_pt[1 - upper] = pt_held[level]
        for half in range(2):
            points = pair_pt[half].astype(F32)
            right_ref[half] = columns_form(points, width, False).astype(BF)
            pair_rows[half * SKEL : (half + 1) * SKEL, :] = columns_form(points, width, True).T
        pick_rows(lambda at: merge_ref[level, at], pair_rows, skel_ref, index_ref)
        pt_ref[level + 1] = (skel_ref[...].T[:features] * 0.5).astype(BF)
        pt_copy(level + 1).start()
        left = skel_ref[...].astype(BF)
        index = index_ref[...]
        table = kept_table(index, 2 * SKEL)
        wide = jnp.concatenate([index] * (SKEL // LANES), axis=1)
        lanes = lax.broadcasted_iota(jnp.int32, wide.shape, 1)
        for half in range(2):
            dense = dense_of(jnp.dot(left, right_ref[half], preferred_element_type=F32), features)
            share = kept_row(table, half * SKEL, SKEL) / jnp.sum(dense, axis=0, keepdims=True)
            spread_ref[half] = jnp.where(wide == lanes + half * SKEL, 1.0, dense * share).astype(BF)

    def merge_weights(level):
        upper = bit(level)
        pair_wt[upper] = wt_ref[level]
        pair_wt[1 - upper] = wt_held[level]
        total = sum(
            lax.dot_general(pair_wt[half], spread_ref[half], NT, preferred_element_type=F32)
            for half in range(2)
        )
        wt_ref[level + 1] = total.astype(BF)
        wt_copy(level + 1).start()

    def near_terms(step):
        for one in range(cap):
            target = jnp.maximum(target_ref[one, ahead(step)], 0)
            for start in range(0, leaf, SKEL):
                points = near_ref[step, one, :features, start : start + SKEL].astype(F32)
                near_right_ref[start : start + SKEL, :] = columns_form(points, width, False).T.astype(BF)

            def tile(begin, start):
                def exponent():
                    return jnp.dot(
                        near_right_ref[start : start + SKEL, :],
                        left_ref[target, :, begin : begin + TILE],
                        preferred_element_type=F32,
                    )

                def use(dense):
                    term = jnp.dot(
                        near_ref[step, one, features:, start : start + SKEL],
                        dense,
                        preferred_element_type=F32,
                    )
                    place = near_out_ref.at[step, one, :, begin : begin + TILE]
                    place[...] = term if start == 0 else place[...] + term

                return exponent, use

            run_tiles(features, [
                tile(begin, start)
                for begin in range(0, leaf, TILE)
                for start in range(0, leaf, SKEL)
            ])

    def far_right(level):
        return columns_form(pt_held[level].astype(F32), width, False).T.astype(BF)

    def far_terms(level):
        far_right_ref[...] = far_right(level)

        def tile(one, begin):
            def exponent():
                return jnp.dot(
                    far_right_ref[...],
                    left_ref[one, :, begin : begin + TILE],
                    preferred_element_type=F32,
                )

            def use(dense):
                weight = (wt_held[level].astype(F32) * far_ref[level, 0, one].astype(F32)).astype(BF)
                term = jnp.dot(weight, dense, preferred_element_type=F32)
                place = out_ref.at[one, :, begin : begin + TILE]
                place[...] = term if level == 0 else place[...] + term

            return exponent, use

        run_tiles(features, [
            tile(one, begin) for one in range(leaves) for begin in range(0, leaf, TILE)
        ])

    def near_ready(step):
        if step > 0:
            near_copy(step).wait_recv()
        near_terms(step)

    steps = iter(range(slabs))
    for level in range(levels - 1):
        pt_copy(level).wait_recv()
        merge_points(level)
        step = next(steps, None)
        if step is not None:
            near_ready(step)
        wt_copy(level).wait_recv()
        merge_weights(level)
    far_terms(0)
    for step in steps:
        near_ready(step)
    for level in range(1, levels - 1):
        far_terms(level)
    pt_copy(levels - 1).wait_recv()
    last_right_ref[...] = far_right(levels - 1)
    wt_copy(levels - 1).wait_recv()
    for one in range(leaves):
        last_weight_ref[one] = (
            wt_held[levels - 1].astype(F32) * far_ref[levels - 1, 0, one].astype(F32)
        ).astype(BF)
    for level in range(levels):
        pt_copy(level).wait_send()
        wt_copy(level).wait_send()
    for step in range(1, slabs):
        ask_copy(step).wait_send()
        near_copy(step).wait_send()


def last_kernel(features, slabs, target_in, right_ref, weight_ref, left_ref, near_ref, prior_ref,
                out_in, sum_ref, target_ref, input_sem, out_sem):
    load = pltpu.make_async_copy(target_in, target_ref, input_sem.at[0])
    load.start()
    leaves, _, leaf = left_ref.shape

    def leave(one):
        return pltpu.make_async_copy(
            sum_ref.at[one], out_in.at[:, pl.ds(one * leaf, leaf)], out_sem.at[one]
        )

    def tile(one, begin):
        def exponent():
            return jnp.dot(
                right_ref[...], left_ref[one, :, begin : begin + TILE], preferred_element_type=F32
            )

        def use(dense):
            place = sum_ref.at[one, :, begin : begin + TILE]
            place[...] += jnp.dot(weight_ref[one], dense, preferred_element_type=F32)

        return exponent, use

    sum_ref[...] = prior_ref[...]
    load.wait()
    for step in range(slabs):
        owner = lax.rem(lax.axis_index("task") + step, slabs)
        for one in range(target_ref.shape[0]):
            target = target_ref[one, owner]

            @pl.when(target >= 0)
            def _():
                sum_ref[target] += near_ref[step, one]

    for one in range(leaves):
        run_tiles(features, [tile(one, begin) for begin in range(0, leaf, TILE)])
        leave(one).start()
    for one in range(leaves):
        leave(one).wait()


def in_hbm(value):
    return pltpu.with_memory_space_constraint(value, pltpu.HBM)


def body(points, weights, point_order, node_order, merge_order, far_list, task_target, task_source):
    count, features = points.shape
    columns = weights.shape[1]
    width = features + columns
    levels = far_list.shape[3]
    leaves = far_list.shape[2]
    leaf = count // leaves
    slabs, cap = task_source.shape[2:]
    far = far_list.transpose(0, 3, 1, 2)[0]
    source = task_source[0, 0].T
    target = task_target[0, 0].T
    inputs = (points.T, weights.T, point_order[0, 0], node_order[0, 0], merge_order[0, 0], far, source, target)
    total, near, left, right, weight = pl.pallas_call(
        functools.partial(chain_kernel, features, levels, slabs),
        out_shape=(
            jax.ShapeDtypeStruct((leaves, columns, leaf), F32),
            jax.ShapeDtypeStruct((slabs, cap, columns, leaf), F32),
            jax.ShapeDtypeStruct((leaves, width, leaf), BF),
            jax.ShapeDtypeStruct((SKEL, width), BF),
            jax.ShapeDtypeStruct((leaves, columns, SKEL), BF),
        ),
        in_specs=[HBM] * 8,
        out_specs=(VMEM,) * 5,
        scratch_shapes=[
            pltpu.VMEM((features, count), BF),
            pltpu.VMEM((columns, count), BF),
            pltpu.VMEM((count, width), F32),
            pltpu.VMEM((count, width), F32),
            pltpu.VMEM((count // SKEL, width, SKEL), BF),
            pltpu.VMEM((SKEL, width), F32),
            pltpu.VMEM((SKEL, width), jnp.int32),
            pltpu.VMEM((2, SKEL, SKEL), BF),
            pltpu.VMEM((2, columns, SKEL), BF),
            pltpu.VMEM((columns, SKEL), F32),
            pltpu.VMEM((leaves, width, leaf), BF),
            pltpu.VMEM((levels, features, SKEL), BF),
            pltpu.VMEM((levels, features, SKEL), BF),
            pltpu.VMEM((levels, columns, SKEL), BF),
            pltpu.VMEM((levels, columns, SKEL), BF),
            pltpu.VMEM((2, features, SKEL), BF),
            pltpu.VMEM((2, columns, SKEL), BF),
            pltpu.VMEM((2 * SKEL, width), F32),
            pltpu.VMEM((2, SKEL, SKEL), BF),
            pltpu.VMEM((leaf, width), BF),
            pltpu.VMEM((SKEL, width), BF),
            pltpu.VMEM((slabs, cap, slabs), jnp.int32),
            pltpu.VMEM((slabs, cap, width, leaf), BF),
            pltpu.VMEM((slabs, cap, width, leaf), BF),
            pltpu.SMEM((count,), jnp.int32),
            pltpu.SMEM((count,), jnp.int32),
            pltpu.SMEM((levels - 1, 2 * SKEL), jnp.int32),
            pltpu.SMEM(far.shape, jnp.int32),
            pltpu.SMEM(target.shape, jnp.int32),
            pltpu.VMEM(source.shape, jnp.int32),
            pltpu.SemaphoreType.DMA((8,)),
            pltpu.SemaphoreType.DMA((levels,)),
            pltpu.SemaphoreType.DMA((levels,)),
            pltpu.SemaphoreType.DMA((levels,)),
            pltpu.SemaphoreType.DMA((levels,)),
            pltpu.SemaphoreType.DMA((slabs,)),
            pltpu.SemaphoreType.DMA((slabs,)),
            pltpu.SemaphoreType.DMA((slabs,)),
            pltpu.SemaphoreType.DMA((slabs,)),
        ],
        compiler_params=pltpu.CompilerParams(
            collective_id=0, has_side_effects=True, vmem_limit_bytes=48 << 20
        ),
        name="chain",
    )(*[in_hbm(one) for one in inputs])
    out = pl.pallas_call(
        functools.partial(last_kernel, features, slabs),
        out_shape=jax.ShapeDtypeStruct((columns, count), F32),
        in_specs=[HBM] + [VMEM] * 5,
        out_specs=HBM,
        scratch_shapes=[
            pltpu.VMEM((leaves, columns, leaf), F32),
            pltpu.SMEM(target.shape, jnp.int32),
            pltpu.SemaphoreType.DMA((1,)),
            pltpu.SemaphoreType.DMA((leaves,)),
        ],
        compiler_params=pltpu.CompilerParams(vmem_limit_bytes=48 << 20),
        name="last",
    )(in_hbm(target), right, weight, left, near, total)
    return out.T


def solution(mesh):
    return jax.shard_map(
        body,
        mesh=mesh,
        in_specs=(
            P(("leaf", "task"), None),
            P(("leaf", "task"), None),
            P("leaf", "task", None),
            P("leaf", "task", None),
            P("leaf", "task", None, None),
            P("leaf", "task", None, None),
            P("leaf", "task", None, None),
            P("leaf", "task", None, None),
        ),
        out_specs=P(("leaf", "task"), None),
        check_vma=False,
    )
```

```python
import functools
import math

import jax
import jax.numpy as jnp
from jax import lax
from jax.experimental import pallas as pl
from jax.experimental.pallas import tpu as pltpu
from jax.sharding import PartitionSpec as P

SKEL = 512
KERNEL_SCALE = 1.5
LANES = 128
BF = jnp.bfloat16
F32 = jnp.float32

VMEM = pl.BlockSpec(memory_space=pltpu.VMEM)
HBM = pl.BlockSpec(memory_space=pltpu.HBM)
MESH = pl.DeviceIdType.MESH
NT = (((1,), (1,)), ((), ()))
TILE = 512


def scale_of(features):
    return KERNEL_SCALE / features * math.log2(math.e)


def pieces(norm):
    first = norm.astype(BF).astype(F32)
    left = norm - first
    second = left.astype(BF).astype(F32)
    third = left - second
    return first, second, third


def columns_form(points, width, left):
    features, count = points.shape
    first, second, third = pieces(jnp.sum(points * points, axis=0, keepdims=True))
    lines = lax.broadcasted_iota(jnp.int32, (8, count), 0)
    at = 0 if left else 3
    ones = 3 - at
    tail = jnp.where((lines >= ones) & (lines < ones + 3), 1.0, 0.0)
    tail = jnp.where(lines == at, -first, tail)
    tail = jnp.where(lines == at + 1, -second, tail)
    tail = jnp.where(lines == at + 2, -third, tail)
    rest = jnp.zeros((width - features - 8, count), F32)
    return jnp.concatenate([points + points if left else points, tail, rest], axis=0)


def dense_of(exponent, features):
    return jnp.exp2(exponent * scale_of(features))


def kept_table(index, count):
    lanes = lax.broadcasted_iota(jnp.int32, index.shape, 1)
    high = jnp.where(lax.shift_right_logical(index, 7) == lanes, 1.0, 0.0).astype(BF).T
    low = jnp.where((index & (LANES - 1)) == lanes, 1.0, 0.0).astype(BF)
    return 1.0 - jnp.dot(high, low, preferred_element_type=F32)


def kept_row(table, start, count):
    rows = [table[at : at + 1, :] for at in range(start // LANES, (start + count) // LANES)]
    return jnp.concatenate(rows, axis=1)


def pick_rows(index_of, rows_ref, skel_ref, index_ref):
    width = rows_ref.shape[1]
    for at in range(SKEL):
        index = index_of(at)
        skel_ref[at : at + 1, :] = rows_ref[index][None]
        index_ref[at : at + 1, :] = jnp.full((1, width), index, jnp.int32)


def run_tiles(features, tiles):
    held = None
    for exponent, use in tiles:
        value = exponent()
        if held is not None:
            held[1](dense_of(held[0], features).astype(BF))
        held = (value, use)
    held[1](dense_of(held[0], features).astype(BF))


def chain_kernel(features, levels, slabs, points_in, weights_in, order_in, node_order_in, merge_in,
                 far_in, source_in, target_in,
                 out_ref, near_out_ref, left_ref, last_right_ref, last_weight_ref,
                 points_ref, weights_ref, rows_ref, picked_ref, right_ref, skel_ref, index_ref,
                 dense_ref, total_ref, tree_ref, pt_ref, pt_held, wt_ref, wt_held,
                 pair_pt, pair_wt, pair_rows, spread_ref, near_right_ref, far_right_ref,
                 asked_ref, send_ref, near_ref,
                 order_ref, node_order_ref, merge_ref, far_ref, target_ref, own_ref, source_ref,
                 input_sem, pt_send, pt_recv, wt_send, wt_recv, ask_send, ask_recv, near_send, near_recv):
    loads = [
        pltpu.make_async_copy(source, target, input_sem.at[at])
        for at, (source, target) in enumerate([
            (points_in, points_ref),
            (weights_in, weights_ref),
            (order_in, order_ref),
            (node_order_in, node_order_ref),
            (merge_in, merge_ref),
            (far_in, far_ref),
            (source_in, source_ref),
            (target_in, target_ref),
            (source_in, own_ref),
        ])
    ]
    for load in loads:
        load.start()
    region = lax.axis_index("leaf")
    slab = lax.axis_index("task")
    count = rows_ref.shape[0]
    width = rows_ref.shape[1]
    leaves = left_ref.shape[0]
    leaf = count // leaves
    cap = source_ref.shape[0]
    chunks = count // SKEL

    def bit(level):
        return region // 2**level % 2

    def sibling(level):
        return region + (1 - 2 * bit(level)) * 2**level

    def ahead(step):
        return lax.rem(slab + step, slabs)

    def behind(step):
        return lax.rem(slab + slabs - step, slabs)

    barrier = pltpu.get_barrier_semaphore()
    for level in range(levels):
        pl.semaphore_signal(barrier, inc=1, device_id=(sibling(level), slab), device_id_type=MESH)
    for step in range(1, slabs):
        pl.semaphore_signal(barrier, inc=1, device_id=(region, ahead(step)), device_id_type=MESH)

    def to_sibling(level, source, target, send, recv):
        return pltpu.make_async_remote_copy(
            src_ref=source.at[level],
            dst_ref=target.at[level],
            send_sem=send.at[level],
            recv_sem=recv.at[level],
            device_id=(sibling(level), slab),
            device_id_type=MESH,
        )

    def pt_copy(level):
        return to_sibling(level, pt_ref, pt_held, pt_send, pt_recv)

    def wt_copy(level):
        return to_sibling(level, wt_ref, wt_held, wt_send, wt_recv)

    def ask_copy(step):
        return pltpu.make_async_remote_copy(
            src_ref=source_ref,
            dst_ref=asked_ref.at[step],
            send_sem=ask_send.at[step],
            recv_sem=ask_recv.at[step],
            device_id=(region, ahead(step)),
            device_id_type=MESH,
        )

    def near_copy(step):
        return pltpu.make_async_remote_copy(
            src_ref=send_ref.at[step],
            dst_ref=near_ref.at[step],
            send_sem=near_send.at[step],
            recv_sem=near_recv.at[step],
            device_id=(region, behind(step)),
            device_id_type=MESH,
        )

    for load in loads:
        load.wait()
    for at in range(chunks):
        both = jnp.concatenate(
            [
                points_ref[:, at * SKEL : (at + 1) * SKEL],
                weights_ref[:, at * SKEL : (at + 1) * SKEL],
            ],
            axis=0,
        )
        rows_ref[at * SKEL : (at + 1) * SKEL, :] = both.T.astype(F32)
    pick_rows(lambda at: order_ref[node_order_ref[at]], rows_ref, skel_ref, index_ref)
    skel = skel_ref[...].astype(BF).T.astype(F32)
    pt_ref[0] = skel[:features].astype(BF)
    pl.semaphore_wait(barrier, levels + slabs - 1)
    pt_copy(0).start()
    for step in range(1, slabs):
        ask_copy(step).start()

    left = columns_form(skel[:features], width, True).astype(BF).T
    table = kept_table(index_ref[...], count)
    total_ref[...] = skel[features:]

    def gather(at):
        for inner in range(SKEL):
            picked_ref[at * SKEL + inner : at * SKEL + inner + 1, :] = rows_ref[
                order_ref[at * SKEL + inner]
            ][None]

    def absorb(at):
        total_ref[...] += lax.dot_general(
            weights_ref[:, at * SKEL : (at + 1) * SKEL],
            dense_ref[at % 2],
            NT,
            preferred_element_type=F32,
        )

    for at in range(chunks):
        right = columns_form(points_ref[:, at * SKEL : (at + 1) * SKEL].astype(F32), width, False)
        dense = dense_of(jnp.dot(left, right.astype(BF), preferred_element_type=F32), features)
        if at > 0:
            absorb(at - 1)
        share = kept_row(table, at * SKEL, SKEL) / jnp.sum(dense, axis=0, keepdims=True)
        dense_ref[at % 2] = (dense * share).astype(BF)
        gather(at)
    absorb(chunks - 1)
    wt_ref[0] = total_ref[...].astype(BF)
    wt_copy(0).start()

    for one in range(leaves):
        for start in range(0, leaf, SKEL):
            turn = picked_ref[one * leaf + start : one * leaf + start + SKEL, :].astype(BF).T
            tree_ref[one, :, start : start + SKEL] = turn
            left_ref[one, :, start : start + SKEL] = columns_form(
                turn[:features].astype(F32), width, True
            ).astype(BF)

    def fill(slot_ref, step, table):
        own = lax.broadcasted_iota(jnp.int32, table.shape, 1) == slab
        place = lax.broadcasted_iota(jnp.int32, table.shape, 0)
        for one in range(cap):
            wanted = jnp.max(
                jnp.where(own & (place == one), table, 0).astype(F32), axis=(0, 1), keepdims=True
            )
            slot_ref[step, one] = sum(
                tree_ref[other] * jnp.where(wanted == other, 1.0, 0.0).astype(BF)
                for other in range(leaves)
            )

    for step in range(1, slabs):
        ask_copy(step).wait_recv()
        fill(send_ref, step, asked_ref[step])
        near_copy(step).start()

    def merge_points(level):
        upper = bit(level)
        pair_pt[upper] = pt_ref[level]
        pair_pt[1 - upper] = pt_held[level]
        for half in range(2):
            points = pair_pt[half].astype(F32)
            right_ref[half] = columns_form(points, width, False).astype(BF)
            pair_rows[half * SKEL : (half + 1) * SKEL, :] = columns_form(points, width, True).astype(BF).T.astype(F32)
        pick_rows(lambda at: merge_ref[level, at], pair_rows, skel_ref, index_ref)
        pt_ref[level + 1] = (skel_ref[...] * 0.5).astype(BF).T[:features]
        pt_copy(level + 1).start()
        left = skel_ref[...].astype(BF)
        index = index_ref[...]
        table = kept_table(index, 2 * SKEL)
        wide = jnp.concatenate([index] * (SKEL // LANES), axis=1)
        lanes = lax.broadcasted_iota(jnp.int32, wide.shape, 1)
        for half in range(2):
            dense = dense_of(jnp.dot(left, right_ref[half], preferred_element_type=F32), features)
            share = kept_row(table, half * SKEL, SKEL) / jnp.sum(dense, axis=0, keepdims=True)
            spread_ref[half] = jnp.where(wide == lanes + half * SKEL, 1.0, dense * share).astype(BF)

    def merge_weights(level):
        upper = bit(level)
        pair_wt[upper] = wt_ref[level]
        pair_wt[1 - upper] = wt_held[level]
        total = sum(
            lax.dot_general(pair_wt[half], spread_ref[half], NT, preferred_element_type=F32)
            for half in range(2)
        )
        wt_ref[level + 1] = total.astype(BF)
        wt_copy(level + 1).start()

    def near_terms(step):
        for one in range(cap):
            target = jnp.maximum(target_ref[one, ahead(step)], 0)
            if step == 0:
                origin, place_at = tree_ref, (own_ref[one, slab],)
            else:
                origin, place_at = near_ref, (step, one)
            for start in range(0, leaf, SKEL):
                points = origin[(*place_at, slice(0, features), slice(start, start + SKEL))]
                near_right_ref[start : start + SKEL, :] = columns_form(
                    points.astype(F32), width, False
                ).astype(BF).T

            def tile(begin, start):
                def exponent():
                    return jnp.dot(
                        near_right_ref[start : start + SKEL, :],
                        left_ref[target, :, begin : begin + TILE],
                        preferred_element_type=F32,
                    )

                def use(dense):
                    weight = origin[
                        (*place_at, slice(features, width), slice(start, start + SKEL))
                    ]
                    term = jnp.dot(weight, dense, preferred_element_type=F32)
                    place = near_out_ref.at[step, one, :, begin : begin + TILE]
                    place[...] = term if start == 0 else place[...] + term

                return exponent, use

            run_tiles(features, [
                tile(begin, start)
                for begin in range(0, leaf, TILE)
                for start in range(0, leaf, SKEL)
            ])

    def far_right(level):
        return columns_form(pt_held[level].astype(F32), width, False).astype(BF).T

    def far_terms(level):
        far_right_ref[...] = far_right(level)

        def tile(one, begin):
            def exponent():
                return jnp.dot(
                    far_right_ref[...],
                    left_ref[one, :, begin : begin + TILE],
                    preferred_element_type=F32,
                )

            def use(dense):
                weight = (wt_held[level].astype(F32) * far_ref[level, 0, one].astype(F32)).astype(BF)
                term = jnp.dot(weight, dense, preferred_element_type=F32)
                place = out_ref.at[one, :, begin : begin + TILE]
                place[...] = term if level == 0 else place[...] + term

            return exponent, use

        run_tiles(features, [
            tile(one, begin) for one in range(leaves) for begin in range(0, leaf, TILE)
        ])

    def near_ready(step):
        if step > 0:
            near_copy(step).wait_recv()
        near_terms(step)

    steps = iter(range(slabs))
    for level in range(levels - 1):
        pt_copy(level).wait_recv()
        merge_points(level)
        step = next(steps, None)
        if step is not None:
            near_ready(step)
        wt_copy(level).wait_recv()
        merge_weights(level)
    far_terms(0)
    for step in steps:
        near_ready(step)
    for level in range(1, levels - 1):
        far_terms(level)
    pt_copy(levels - 1).wait_recv()
    last_right_ref[...] = far_right(levels - 1)
    wt_copy(levels - 1).wait_recv()
    for one in range(leaves):
        last_weight_ref[one] = (
            wt_held[levels - 1].astype(F32) * far_ref[levels - 1, 0, one].astype(F32)
        ).astype(BF)
    for level in range(levels):
        pt_copy(level).wait_send()
        wt_copy(level).wait_send()
    for step in range(1, slabs):
        ask_copy(step).wait_send()
        near_copy(step).wait_send()


def last_kernel(features, slabs, target_in, right_ref, weight_ref, left_ref, near_ref, prior_ref,
                out_in, sum_ref, target_ref, input_sem, out_sem):
    load = pltpu.make_async_copy(target_in, target_ref, input_sem.at[0])
    load.start()
    leaves, _, leaf = left_ref.shape

    def leave(one):
        return pltpu.make_async_copy(
            sum_ref.at[one], out_in.at[:, pl.ds(one * leaf, leaf)], out_sem.at[one]
        )

    def tile(one, begin):
        def exponent():
            return jnp.dot(
                right_ref[...], left_ref[one, :, begin : begin + TILE], preferred_element_type=F32
            )

        def use(dense):
            place = sum_ref.at[one, :, begin : begin + TILE]
            place[...] += jnp.dot(weight_ref[one], dense, preferred_element_type=F32)

        return exponent, use

    sum_ref[...] = prior_ref[...]
    for one in range(leaves):
        run_tiles(features, [tile(one, begin) for begin in range(0, leaf, TILE)])
        if one == 0:
            load.wait()
            for step in range(slabs):
                owner = lax.rem(lax.axis_index("task") + step, slabs)
                for slot in range(target_ref.shape[0]):
                    target = target_ref[slot, owner]

                    @pl.when(target >= 0)
                    def _(step=step, slot=slot, target=target):
                        sum_ref[target] += near_ref[step, slot]

        leave(one).start()
    for one in range(leaves):
        leave(one).wait()


def in_hbm(value):
    return pltpu.with_memory_space_constraint(value, pltpu.HBM)


def body(points, weights, point_order, node_order, merge_order, far_list, task_target, task_source):
    count, features = points.shape
    columns = weights.shape[1]
    width = features + columns
    levels = far_list.shape[3]
    leaves = far_list.shape[2]
    leaf = count // leaves
    slabs, cap = task_source.shape[2:]
    far = far_list.transpose(0, 3, 1, 2)[0]
    source = task_source[0, 0].T
    target = task_target[0, 0].T
    inputs = (points.T, weights.T, point_order[0, 0], node_order[0, 0], merge_order[0, 0], far, source, target)
    total, near, left, right, weight = pl.pallas_call(
        functools.partial(chain_kernel, features, levels, slabs),
        out_shape=(
            jax.ShapeDtypeStruct((leaves, columns, leaf), F32),
            jax.ShapeDtypeStruct((slabs, cap, columns, leaf), F32),
            jax.ShapeDtypeStruct((leaves, width, leaf), BF),
            jax.ShapeDtypeStruct((SKEL, width), BF),
            jax.ShapeDtypeStruct((leaves, columns, SKEL), BF),
        ),
        in_specs=[HBM] * 8,
        out_specs=(VMEM,) * 5,
        scratch_shapes=[
            pltpu.VMEM((features, count), BF),
            pltpu.VMEM((columns, count), BF),
            pltpu.VMEM((count, width), F32),
            pltpu.VMEM((count, width), F32),
            pltpu.VMEM((2, width, SKEL), BF),
            pltpu.VMEM((SKEL, width), F32),
            pltpu.VMEM((SKEL, width), jnp.int32),
            pltpu.VMEM((2, SKEL, SKEL), BF),
            pltpu.VMEM((columns, SKEL), F32),
            pltpu.VMEM((leaves, width, leaf), BF),
            pltpu.VMEM((levels, features, SKEL), BF),
            pltpu.VMEM((levels, features, SKEL), BF),
            pltpu.VMEM((levels, columns, SKEL), BF),
            pltpu.VMEM((levels, columns, SKEL), BF),
            pltpu.VMEM((2, features, SKEL), BF),
            pltpu.VMEM((2, columns, SKEL), BF),
            pltpu.VMEM((2 * SKEL, width), F32),
            pltpu.VMEM((2, SKEL, SKEL), BF),
            pltpu.VMEM((leaf, width), BF),
            pltpu.VMEM((SKEL, width), BF),
            pltpu.VMEM((slabs, cap, slabs), jnp.int32),
            pltpu.VMEM((slabs, cap, width, leaf), BF),
            pltpu.VMEM((slabs, cap, width, leaf), BF),
            pltpu.SMEM((count,), jnp.int32),
            pltpu.SMEM((count,), jnp.int32),
            pltpu.SMEM((levels - 1, 2 * SKEL), jnp.int32),
            pltpu.SMEM(far.shape, jnp.int32),
            pltpu.SMEM(target.shape, jnp.int32),
            pltpu.SMEM(source.shape, jnp.int32),
            pltpu.VMEM(source.shape, jnp.int32),
            pltpu.SemaphoreType.DMA((9,)),
            pltpu.SemaphoreType.DMA((levels,)),
            pltpu.SemaphoreType.DMA((levels,)),
            pltpu.SemaphoreType.DMA((levels,)),
            pltpu.SemaphoreType.DMA((levels,)),
            pltpu.SemaphoreType.DMA((slabs,)),
            pltpu.SemaphoreType.DMA((slabs,)),
            pltpu.SemaphoreType.DMA((slabs,)),
            pltpu.SemaphoreType.DMA((slabs,)),
        ],
        compiler_params=pltpu.CompilerParams(
            collective_id=0, has_side_effects=True, vmem_limit_bytes=48 << 20
        ),
        name="chain",
    )(*[in_hbm(one) for one in inputs])
    out = pl.pallas_call(
        functools.partial(last_kernel, features, slabs),
        out_shape=jax.ShapeDtypeStruct((columns, count), F32),
        in_specs=[HBM] + [VMEM] * 5,
        out_specs=HBM,
        scratch_shapes=[
            pltpu.VMEM((leaves, columns, leaf), F32),
            pltpu.SMEM(target.shape, jnp.int32),
            pltpu.SemaphoreType.DMA((1,)),
            pltpu.SemaphoreType.DMA((leaves,)),
        ],
        compiler_params=pltpu.CompilerParams(vmem_limit_bytes=48 << 20),
        name="last",
    )(in_hbm(target), right, weight, left, near, total)
    return out.T


def solution(mesh):
    return jax.shard_map(
        body,
        mesh=mesh,
        in_specs=(
            P(("leaf", "task"), None),
            P(("leaf", "task"), None),
            P("leaf", "task", None),
            P("leaf", "task", None),
            P("leaf", "task", None, None),
            P("leaf", "task", None, None),
            P("leaf", "task", None, None),
            P("leaf", "task", None, None),
        ),
        out_specs=P(("leaf", "task"), None),
        check_vma=False,
    )
```

```python
import functools
import math

import jax
import jax.numpy as jnp
from jax import lax
from jax.experimental import pallas as pl
from jax.experimental.pallas import tpu as pltpu
from jax.sharding import PartitionSpec as P

SKEL = 512
KERNEL_SCALE = 1.5
LANES = 128
BF = jnp.bfloat16
F32 = jnp.float32

VMEM = pl.BlockSpec(memory_space=pltpu.VMEM)
HBM = pl.BlockSpec(memory_space=pltpu.HBM)
MESH = pl.DeviceIdType.MESH
NT = (((1,), (1,)), ((), ()))
TILE = 512
HALF = 256


def scale_of(features):
    return KERNEL_SCALE / features * math.log2(math.e)


def pieces(norm):
    first = norm.astype(BF).astype(F32)
    left = norm - first
    second = left.astype(BF).astype(F32)
    third = left - second
    return first, second, third


def columns_form(points, width, left):
    features, count = points.shape
    first, second, third = pieces(jnp.sum(points * points, axis=0, keepdims=True))
    lines = lax.broadcasted_iota(jnp.int32, (8, count), 0)
    at = 0 if left else 3
    ones = 3 - at
    tail = jnp.where((lines >= ones) & (lines < ones + 3), 1.0, 0.0)
    tail = jnp.where(lines == at, -first, tail)
    tail = jnp.where(lines == at + 1, -second, tail)
    tail = jnp.where(lines == at + 2, -third, tail)
    rest = jnp.zeros((width - features - 8, count), F32)
    return jnp.concatenate([points + points if left else points, tail, rest], axis=0)


def dense_of(exponent, features):
    return jnp.exp2(exponent * scale_of(features))


def kept_table(index, count):
    lanes = lax.broadcasted_iota(jnp.int32, index.shape, 1)
    high = jnp.where(lax.shift_right_logical(index, 7) == lanes, 1.0, 0.0).astype(BF).T
    low = jnp.where((index & (LANES - 1)) == lanes, 1.0, 0.0).astype(BF)
    return 1.0 - jnp.dot(high, low, preferred_element_type=F32)


def kept_row(table, start, count):
    rows = [table[at : at + 1, :] for at in range(start // LANES, (start + count) // LANES)]
    return jnp.concatenate(rows, axis=1)


def pick_rows(index_of, rows_ref, skel_ref, index_ref, start, count):
    width = rows_ref.shape[1]
    for at in range(start, start + count):
        index = index_of(at)
        skel_ref[at : at + 1, :] = rows_ref[index][None]
        index_ref[at : at + 1, :] = jnp.full((1, width), index, jnp.int32)


def partner_of(slab, step):
    flips = [1 << at for at in range(step.bit_length()) if step >> at & 1]
    return slab + sum((1 - 2 * (slab // flip % 2)) * flip for flip in flips)


def tile_steps(features, tiles):
    held = []

    def step(tile):
        value = tile[0]() if tile else None
        if held:
            exponent, use = held.pop()
            use(dense_of(exponent, features))
        if tile:
            held.append((value, tile[1]))

    return [functools.partial(step, tile) for tile in [*tiles, None]]


def run(*streams):
    marked = [
        ((at + 0.5) / len(stream), which, step)
        for which, stream in enumerate(streams)
        for at, step in enumerate(stream)
    ]
    for _, _, step in sorted(marked, key=lambda one: one[:2]):
        step()


def chain_kernel(features, levels, slabs, points_in, weights_in, order_in, node_order_in, merge_in,
                 far_in, source_in, target_in,
                 out_ref, near_out_ref, left_ref, last_right_ref, last_weight_ref,
                 points_ref, weights_ref, rows_ref, picked_ref, right_ref, skel_ref, index_ref,
                 left_rows_ref, table_ref, dense_ref, share_ref, total_ref, tree_ref, pt_ref, pt_held, wt_ref, wt_held,
                 pair_pt, pair_wt, pair_rows, spread_ref, near_right_ref, far_right_ref,
                 asked_ref, send_ref, near_ref,
                 order_ref, node_order_ref, merge_ref, far_ref, target_ref, own_ref, source_ref,
                 input_sem, pt_send, pt_recv, wt_send, wt_recv, ask_send, ask_recv, near_send, near_recv):
    loads = [
        pltpu.make_async_copy(source, target, input_sem.at[at])
        for at, (source, target) in enumerate([
            (points_in, points_ref),
            (weights_in, weights_ref),
            (order_in, order_ref),
            (node_order_in, node_order_ref),
            (merge_in, merge_ref),
            (far_in, far_ref),
            (source_in, source_ref),
            (target_in, target_ref),
            (source_in, own_ref),
        ])
    ]
    for load in loads:
        load.start()
    region = lax.axis_index("leaf")
    slab = lax.axis_index("task")
    count = rows_ref.shape[0]
    width = rows_ref.shape[1]
    leaves = left_ref.shape[0]
    leaf = count // leaves
    cap = source_ref.shape[0]
    chunks = count // SKEL

    def bit(level):
        return region // 2**level % 2

    def sibling(level):
        return region + (1 - 2 * bit(level)) * 2**level

    def partner(step):
        return partner_of(slab, step)

    barrier = pltpu.get_barrier_semaphore()
    for level in range(levels):
        pl.semaphore_signal(barrier, inc=1, device_id=(sibling(level), slab), device_id_type=MESH)
    for step in range(1, slabs):
        pl.semaphore_signal(barrier, inc=1, device_id=(region, partner(step)), device_id_type=MESH)

    def to_sibling(level, source, target, send, recv):
        return pltpu.make_async_remote_copy(
            src_ref=source.at[level],
            dst_ref=target.at[level],
            send_sem=send.at[level],
            recv_sem=recv.at[level],
            device_id=(sibling(level), slab),
            device_id_type=MESH,
        )

    def pt_copy(level):
        return to_sibling(level, pt_ref, pt_held, pt_send, pt_recv)

    def wt_copy(level):
        return to_sibling(level, wt_ref, wt_held, wt_send, wt_recv)

    def ask_copy(step):
        return pltpu.make_async_remote_copy(
            src_ref=source_ref,
            dst_ref=asked_ref.at[step],
            send_sem=ask_send.at[step],
            recv_sem=ask_recv.at[step],
            device_id=(region, partner(step)),
            device_id_type=MESH,
        )

    def near_copy(step):
        return pltpu.make_async_remote_copy(
            src_ref=send_ref.at[step],
            dst_ref=near_ref.at[step],
            send_sem=near_send.at[step],
            recv_sem=near_recv.at[step],
            device_id=(region, partner(step)),
            device_id_type=MESH,
        )

    for load in loads:
        load.wait()
    for at in range(chunks):
        both = jnp.concatenate(
            [
                points_ref[:, at * SKEL : (at + 1) * SKEL],
                weights_ref[:, at * SKEL : (at + 1) * SKEL],
            ],
            axis=0,
        )
        rows_ref[at * SKEL : (at + 1) * SKEL, :] = both.T.astype(F32)
    pick_rows(lambda at: order_ref[node_order_ref[at]], rows_ref, skel_ref, index_ref, 0, SKEL)
    skel = skel_ref[...].astype(BF).T.astype(F32)
    pt_ref[0] = skel[:features].astype(BF)
    pl.semaphore_wait(barrier, levels + slabs - 1)
    pt_copy(0).start()
    for step in range(1, slabs):
        ask_copy(step).start()

    left_rows_ref[...] = columns_form(skel[:features], width, True).astype(BF).T
    table_ref[...] = kept_table(index_ref[...], count)
    total_ref[...] = skel[features:]

    def zero_dense(at):
        columns = slice(at * SKEL, (at + 1) * SKEL)
        right = columns_form(points_ref[:, columns].astype(F32), width, False).astype(BF)
        dense = dense_of(
            jnp.dot(left_rows_ref[...], right, preferred_element_type=F32), features
        )
        dense_ref[at % 2] = dense
        share_ref[at % 2] = kept_row(table_ref, at * SKEL, SKEL) / jnp.sum(
            dense, axis=0, keepdims=True
        )

    def zero_spread(at):
        total_ref[...] += lax.dot_general(
            weights_ref[:, at * SKEL : (at + 1) * SKEL],
            (dense_ref[at % 2] * share_ref[at % 2]).astype(BF),
            NT,
            preferred_element_type=F32,
        )

    def gather(at):
        for row in range(at * SKEL, (at + 1) * SKEL):
            picked_ref[row : row + 1, :] = rows_ref[order_ref[row]][None]

    def to_tree(at):
        one, begin = at * SKEL // leaf, at * SKEL % leaf
        turn = picked_ref[at * SKEL : (at + 1) * SKEL, :].astype(BF).T
        tree_ref[one, :, begin : begin + SKEL] = turn
        left_ref[one, :, begin : begin + SKEL] = columns_form(
            turn[:features].astype(F32), width, True
        ).astype(BF)

    for at in range(chunks + 1):
        if at < chunks:
            zero_dense(at)
        if at > 0:
            zero_spread(at - 1)
            to_tree(at - 1)
        if at < chunks:
            gather(at)

    wt_ref[0] = total_ref[...].astype(BF)
    wt_copy(0).start()

    def fill(slot_ref, step, table):
        own = lax.broadcasted_iota(jnp.int32, table.shape, 1) == slab
        place = lax.broadcasted_iota(jnp.int32, table.shape, 0)
        for one in range(cap):
            wanted = jnp.max(
                jnp.where(own & (place == one), table, 0).astype(F32), axis=(0, 1), keepdims=True
            )
            slot_ref[step, one] = sum(
                tree_ref[other] * jnp.where(wanted == other, 1.0, 0.0).astype(BF)
                for other in range(leaves)
            )

    for step in reversed(range(1, slabs)):
        ask_copy(step).wait_recv()
        fill(send_ref, step, asked_ref[step])
        near_copy(step).start()

    def merge_points(level):
        upper = bit(level)

        def pair():
            pair_pt[upper] = pt_ref[level]
            pair_pt[1 - upper] = pt_held[level]
            for half in range(2):
                points = pair_pt[half].astype(F32)
                right_ref[half] = columns_form(points, width, False).astype(BF)
                pair_rows[half * SKEL : (half + 1) * SKEL, :] = (
                    columns_form(points, width, True).astype(BF).T.astype(F32)
                )

        def pick(start):
            pick_rows(
                lambda at: merge_ref[level, at], pair_rows, skel_ref, index_ref, start, HALF
            )

        def leave():
            left_rows_ref[...] = skel_ref[...].astype(BF)
            pt_ref[level + 1] = (skel_ref[...] * 0.5).astype(BF).T[:features]
            pt_copy(level + 1).start()
            table_ref[...] = kept_table(index_ref[...], 2 * SKEL)

        def dense(half):
            value = dense_of(
                jnp.dot(left_rows_ref[...], right_ref[half], preferred_element_type=F32), features
            )
            dense_ref[half] = value
            share_ref[half] = kept_row(table_ref, half * SKEL, SKEL) / jnp.sum(
                value, axis=0, keepdims=True
            )

        def spread(half):
            index = index_ref[...]
            for start in range(0, SKEL, LANES):
                columns = slice(start, start + LANES)
                lanes = lax.broadcasted_iota(jnp.int32, index.shape, 1) + (half * SKEL + start)
                spread_ref[half, :, columns] = jnp.where(
                    index == lanes, 1.0, dense_ref[half, :, columns] * share_ref[half, :, columns]
                ).astype(BF)

        return [
            [pair],
            [functools.partial(pick, 0)],
            [functools.partial(pick, HALF)],
            [leave, functools.partial(dense, 0)],
            [functools.partial(spread, 0), functools.partial(dense, 1)],
            [functools.partial(spread, 1)],
        ]

    def beside(parts, turns, tiles):
        for at, part in enumerate(parts):
            share = turns if at == 0 else tile_steps(
                features,
                tiles[len(tiles) * (at - 1) // (len(parts) - 1) : len(tiles) * at // (len(parts) - 1)],
            )

            run(part, share)

    def merge_weights(level):
        upper = bit(level)
        pair_wt[upper] = wt_ref[level]
        pair_wt[1 - upper] = wt_held[level]
        total = sum(
            lax.dot_general(pair_wt[half], spread_ref[half], NT, preferred_element_type=F32)
            for half in range(2)
        )
        wt_ref[level + 1] = total.astype(BF)
        wt_copy(level + 1).start()

    def near_terms(step):
        slots = [near_slot(step, one) for one in range(cap)]
        return sum([slot[0] for slot in slots], []), sum([slot[1] for slot in slots], [])

    def near_slot(step, one):
        target = jnp.maximum(target_ref[one, partner(step)], 0)
        if step == 0:
            origin, place_at = tree_ref, (own_ref[one, slab],)
        else:
            origin, place_at = near_ref, (step, one)

        def turn(start):
            points = origin[(*place_at, slice(0, features), slice(start, start + SKEL))]
            near_right_ref[one, start : start + SKEL, :] = columns_form(
                points.astype(F32), width, False
            ).astype(BF).T

        def tile(begin, start):
            def exponent():
                return jnp.dot(
                    near_right_ref[one, start : start + SKEL, :],
                    left_ref[target, :, begin : begin + TILE],
                    preferred_element_type=F32,
                )

            def use(dense):
                weight = origin[(*place_at, slice(features, width), slice(start, start + SKEL))]
                term = jnp.dot(weight, dense.astype(BF), preferred_element_type=F32)
                place = near_out_ref.at[step, one, :, begin : begin + TILE]
                place[...] = term if start == 0 else place[...] + term

            return exponent, use

        return (
            [functools.partial(turn, start) for start in range(0, leaf, SKEL)],
            [
                tile(begin, start)
                for begin in range(0, leaf, TILE)
                for start in range(0, leaf, SKEL)
            ],
        )

    def far_right(level):
        return columns_form(pt_held[level].astype(F32), width, False).astype(BF).T

    def far_terms(level):
        def turn():
            far_right_ref[...] = far_right(level)

        def tile(one, begin):
            def exponent():
                return jnp.dot(
                    far_right_ref[...],
                    left_ref[one, :, begin : begin + TILE],
                    preferred_element_type=F32,
                )

            def use(dense):
                weight = (wt_held[level].astype(F32) * far_ref[level, 0, one].astype(F32)).astype(BF)
                term = jnp.dot(weight, dense.astype(BF), preferred_element_type=F32)
                place = out_ref.at[one, :, begin : begin + TILE]
                place[...] = term if level == 0 else place[...] + term

            return exponent, use

        return (
            [turn],
            [tile(one, begin) for one in range(leaves) for begin in range(0, leaf, TILE)],
        )

    def alone(terms):
        turns, tiles = terms
        run([*turns, *tile_steps(features, tiles)])

    for level in range(levels - 1):
        pt_copy(level).wait_recv()
        if level == 0:
            beside(merge_points(level), *near_terms(0))
            if slabs > 1:
                near_copy(1).wait_recv()
                alone(near_terms(1))
        else:
            beside(merge_points(level), *far_terms(level - 1))
        wt_copy(level).wait_recv()
        merge_weights(level)
    alone(far_terms(levels - 2))
    for step in reversed(range(2, slabs)):
        near_copy(step).wait_recv()
        alone(near_terms(step))
    pt_copy(levels - 1).wait_recv()
    last_right_ref[...] = far_right(levels - 1)
    wt_copy(levels - 1).wait_recv()
    for one in range(leaves):
        last_weight_ref[one] = (
            wt_held[levels - 1].astype(F32) * far_ref[levels - 1, 0, one].astype(F32)
        ).astype(BF)
    for level in range(levels):
        pt_copy(level).wait_send()
        wt_copy(level).wait_send()
    for step in range(1, slabs):
        ask_copy(step).wait_send()
        near_copy(step).wait_send()


def last_kernel(features, slabs, target_in, right_ref, weight_ref, left_ref, near_ref, prior_ref,
                out_in, sum_ref, target_ref, input_sem, out_sem):
    load = pltpu.make_async_copy(target_in, target_ref, input_sem.at[0])
    load.start()
    leaves, _, leaf = left_ref.shape

    def leave(one):
        return pltpu.make_async_copy(
            sum_ref.at[one], out_in.at[:, pl.ds(one * leaf, leaf)], out_sem.at[one]
        )

    def tile(one, begin):
        def exponent():
            return jnp.dot(
                right_ref[...], left_ref[one, :, begin : begin + TILE], preferred_element_type=F32
            )

        def use(dense):
            place = sum_ref.at[one, :, begin : begin + TILE]
            place[...] += jnp.dot(weight_ref[one], dense.astype(BF), preferred_element_type=F32)

        return exponent, use

    sum_ref[...] = prior_ref[...]
    for one in range(leaves):
        run(tile_steps(features, [tile(one, begin) for begin in range(0, leaf, TILE)]))
        if one == 0:
            load.wait()
            for step in range(slabs):
                owner = partner_of(lax.axis_index("task"), step)
                for slot in range(target_ref.shape[0]):
                    target = target_ref[slot, owner]

                    @pl.when(target >= 0)
                    def _(step=step, slot=slot, target=target):
                        sum_ref[target] += near_ref[step, slot]

        leave(one).start()
    for one in range(leaves):
        leave(one).wait()


def in_hbm(value):
    return pltpu.with_memory_space_constraint(value, pltpu.HBM)


def body(points, weights, point_order, node_order, merge_order, far_list, task_target, task_source):
    count, features = points.shape
    columns = weights.shape[1]
    width = features + columns
    levels = far_list.shape[3]
    leaves = far_list.shape[2]
    leaf = count // leaves
    slabs, cap = task_source.shape[2:]
    far = far_list.transpose(0, 3, 1, 2)[0]
    source = task_source[0, 0].T
    target = task_target[0, 0].T
    inputs = (points.T, weights.T, point_order[0, 0], node_order[0, 0], merge_order[0, 0], far, source, target)
    total, near, left, right, weight = pl.pallas_call(
        functools.partial(chain_kernel, features, levels, slabs),
        out_shape=(
            jax.ShapeDtypeStruct((leaves, columns, leaf), F32),
            jax.ShapeDtypeStruct((slabs, cap, columns, leaf), F32),
            jax.ShapeDtypeStruct((leaves, width, leaf), BF),
            jax.ShapeDtypeStruct((SKEL, width), BF),
            jax.ShapeDtypeStruct((leaves, columns, SKEL), BF),
        ),
        in_specs=[HBM] * 8,
        out_specs=(VMEM,) * 5,
        scratch_shapes=[
            pltpu.VMEM((features, count), BF),
            pltpu.VMEM((columns, count), BF),
            pltpu.VMEM((count, width), F32),
            pltpu.VMEM((count, width), F32),
            pltpu.VMEM((2, width, SKEL), BF),
            pltpu.VMEM((SKEL, width), F32),
            pltpu.VMEM((SKEL, width), jnp.int32),
            pltpu.VMEM((SKEL, width), BF),
            pltpu.VMEM((LANES, LANES), F32),
            pltpu.VMEM((2, SKEL, SKEL), F32),
            pltpu.VMEM((2, 1, SKEL), F32),
            pltpu.VMEM((columns, SKEL), F32),
            pltpu.VMEM((leaves, width, leaf), BF),
            pltpu.VMEM((levels, features, SKEL), BF),
            pltpu.VMEM((levels, features, SKEL), BF),
            pltpu.VMEM((levels, columns, SKEL), BF),
            pltpu.VMEM((levels, columns, SKEL), BF),
            pltpu.VMEM((2, features, SKEL), BF),
            pltpu.VMEM((2, columns, SKEL), BF),
            pltpu.VMEM((2 * SKEL, width), F32),
            pltpu.VMEM((2, SKEL, SKEL), BF),
            pltpu.VMEM((cap, leaf, width), BF),
            pltpu.VMEM((SKEL, width), BF),
            pltpu.VMEM((slabs, cap, slabs), jnp.int32),
            pltpu.VMEM((slabs, cap, width, leaf), BF),
            pltpu.VMEM((slabs, cap, width, leaf), BF),
            pltpu.SMEM((count,), jnp.int32),
            pltpu.SMEM((count,), jnp.int32),
            pltpu.SMEM((levels - 1, 2 * SKEL), jnp.int32),
            pltpu.SMEM(far.shape, jnp.int32),
            pltpu.SMEM(target.shape, jnp.int32),
            pltpu.SMEM(source.shape, jnp.int32),
            pltpu.VMEM(source.shape, jnp.int32),
            pltpu.SemaphoreType.DMA((9,)),
            pltpu.SemaphoreType.DMA((levels,)),
            pltpu.SemaphoreType.DMA((levels,)),
            pltpu.SemaphoreType.DMA((levels,)),
            pltpu.SemaphoreType.DMA((levels,)),
            pltpu.SemaphoreType.DMA((slabs,)),
            pltpu.SemaphoreType.DMA((slabs,)),
            pltpu.SemaphoreType.DMA((slabs,)),
            pltpu.SemaphoreType.DMA((slabs,)),
        ],
        compiler_params=pltpu.CompilerParams(
            collective_id=0, has_side_effects=True, vmem_limit_bytes=48 << 20
        ),
        name="chain",
    )(*[in_hbm(one) for one in inputs])
    out = pl.pallas_call(
        functools.partial(last_kernel, features, slabs),
        out_shape=jax.ShapeDtypeStruct((columns, count), F32),
        in_specs=[HBM] + [VMEM] * 5,
        out_specs=HBM,
        scratch_shapes=[
            pltpu.VMEM((leaves, columns, leaf), F32),
            pltpu.SMEM(target.shape, jnp.int32),
            pltpu.SemaphoreType.DMA((1,)),
            pltpu.SemaphoreType.DMA((leaves,)),
        ],
        compiler_params=pltpu.CompilerParams(vmem_limit_bytes=48 << 20),
        name="last",
    )(in_hbm(target), right, weight, left, near, total)
    return out.T


def solution(mesh):
    return jax.shard_map(
        body,
        mesh=mesh,
        in_specs=(
            P(("leaf", "task"), None),
            P(("leaf", "task"), None),
            P("leaf", "task", None),
            P("leaf", "task", None),
            P("leaf", "task", None, None),
            P("leaf", "task", None, None),
            P("leaf", "task", None, None),
            P("leaf", "task", None, None),
        ),
        out_specs=P(("leaf", "task"), None),
        check_vma=False,
    )
```

```python
import functools
import math

import jax
import jax.numpy as jnp
from jax import lax
from jax.experimental import pallas as pl
from jax.experimental.pallas import tpu as pltpu
from jax.sharding import PartitionSpec as P

SKEL = 512
KERNEL_SCALE = 1.5
LANES = 128
BF = jnp.bfloat16
F32 = jnp.float32

VMEM = pl.BlockSpec(memory_space=pltpu.VMEM)
HBM = pl.BlockSpec(memory_space=pltpu.HBM)
MESH = pl.DeviceIdType.MESH
NT = (((1,), (1,)), ((), ()))
TILE = 512
HALF = 256


def scale_of(features):
    return KERNEL_SCALE / features * math.log2(math.e)


def pieces(norm):
    first = norm.astype(BF).astype(F32)
    left = norm - first
    second = left.astype(BF).astype(F32)
    third = left - second
    return first, second, third


def columns_form(points, width, left):
    features, count = points.shape
    first, second, third = pieces(jnp.sum(points * points, axis=0, keepdims=True))
    lines = lax.broadcasted_iota(jnp.int32, (8, count), 0)
    at = 0 if left else 3
    ones = 3 - at
    tail = jnp.where((lines >= ones) & (lines < ones + 3), 1.0, 0.0)
    tail = jnp.where(lines == at, -first, tail)
    tail = jnp.where(lines == at + 1, -second, tail)
    tail = jnp.where(lines == at + 2, -third, tail)
    rest = jnp.zeros((width - features - 8, count), F32)
    return jnp.concatenate([points + points if left else points, tail, rest], axis=0)


def dense_of(exponent, features):
    return jnp.exp2(exponent * scale_of(features))


def kept_table(index, count):
    lanes = lax.broadcasted_iota(jnp.int32, index.shape, 1)
    high = jnp.where(lax.shift_right_logical(index, 7) == lanes, 1.0, 0.0).astype(BF).T
    low = jnp.where((index & (LANES - 1)) == lanes, 1.0, 0.0).astype(BF)
    return 1.0 - jnp.dot(high, low, preferred_element_type=F32)


def kept_row(table, start, count):
    rows = [table[at : at + 1, :] for at in range(start // LANES, (start + count) // LANES)]
    return jnp.concatenate(rows, axis=1)


def pick_rows(index_of, rows_ref, skel_ref, index_ref, start, count):
    width = rows_ref.shape[1]
    for at in range(start, start + count):
        index = index_of(at)
        skel_ref[at : at + 1, :] = rows_ref[index][None]
        index_ref[at : at + 1, :] = jnp.full((1, width), index, jnp.int32)


def partner_of(slab, step):
    flips = [1 << at for at in range(step.bit_length()) if step >> at & 1]
    return slab + sum((1 - 2 * (slab // flip % 2)) * flip for flip in flips)


def tile_steps(features, tiles):
    held = []

    def step(tile):
        value = tile[0]() if tile else None
        if held:
            exponent, use = held.pop()
            use(dense_of(exponent, features))
        if tile:
            held.append((value, tile[1]))

    return [functools.partial(step, tile) for tile in [*tiles, None]]


def run(*streams):
    marked = [
        ((at + 0.5) / len(stream), which, step)
        for which, stream in enumerate(streams)
        for at, step in enumerate(stream)
    ]
    for _, _, step in sorted(marked, key=lambda one: one[:2]):
        step()


def chain_kernel(features, levels, slabs, points_in, weights_in, order_in, node_order_in, merge_in,
                 far_in, source_in, target_in,
                 out_ref, near_out_ref, left_ref, last_right_ref, last_weight_ref, near_ref,
                 points_ref, weights_ref, rows_ref, picked_ref, right_ref, skel_ref, index_ref,
                 left_rows_ref, table_ref, dense_ref, share_ref, total_ref, tree_ref, pt_ref, pt_held, wt_ref, wt_held,
                 pair_pt, pair_wt, pair_rows, spread_ref, near_right_ref, far_right_ref,
                 asked_ref, send_ref,
                 order_ref, node_order_ref, merge_ref, far_ref, target_ref, own_ref, source_ref,
                 input_sem, pt_send, pt_recv, wt_send, wt_recv, ask_send, ask_recv, near_send, near_recv):
    loads = [
        pltpu.make_async_copy(source, target, input_sem.at[at])
        for at, (source, target) in enumerate([
            (points_in, points_ref),
            (weights_in, weights_ref),
            (order_in, order_ref),
            (node_order_in, node_order_ref),
            (merge_in, merge_ref),
            (far_in, far_ref),
            (source_in, source_ref),
            (target_in, target_ref),
            (source_in, own_ref),
        ])
    ]
    for load in loads:
        load.start()
    region = lax.axis_index("leaf")
    slab = lax.axis_index("task")
    count = rows_ref.shape[0]
    width = rows_ref.shape[1]
    leaves = left_ref.shape[0]
    leaf = count // leaves
    cap = source_ref.shape[0]
    chunks = count // SKEL

    def bit(level):
        return region // 2**level % 2

    def sibling(level):
        return region + (1 - 2 * bit(level)) * 2**level

    def partner(step):
        return partner_of(slab, step)

    barrier = pltpu.get_barrier_semaphore()
    for level in range(levels):
        pl.semaphore_signal(barrier, inc=1, device_id=(sibling(level), slab), device_id_type=MESH)
    for step in range(1, slabs):
        pl.semaphore_signal(barrier, inc=1, device_id=(region, partner(step)), device_id_type=MESH)

    def to_sibling(level, source, target, send, recv):
        return pltpu.make_async_remote_copy(
            src_ref=source.at[level],
            dst_ref=target.at[level],
            send_sem=send.at[level],
            recv_sem=recv.at[level],
            device_id=(sibling(level), slab),
            device_id_type=MESH,
        )

    def pt_copy(level):
        return to_sibling(level, pt_ref, pt_held, pt_send, pt_recv)

    def wt_copy(level):
        return to_sibling(level, wt_ref, wt_held, wt_send, wt_recv)

    def ask_copy(step):
        return pltpu.make_async_remote_copy(
            src_ref=source_ref,
            dst_ref=asked_ref.at[step],
            send_sem=ask_send.at[step],
            recv_sem=ask_recv.at[step],
            device_id=(region, partner(step)),
            device_id_type=MESH,
        )

    def near_copy(step):
        return pltpu.make_async_remote_copy(
            src_ref=send_ref.at[step],
            dst_ref=near_ref.at[step],
            send_sem=near_send.at[step],
            recv_sem=near_recv.at[step],
            device_id=(region, partner(step)),
            device_id_type=MESH,
        )

    for load in loads:
        load.wait()
    for at in range(chunks):
        both = jnp.concatenate(
            [
                points_ref[:, at * SKEL : (at + 1) * SKEL],
                weights_ref[:, at * SKEL : (at + 1) * SKEL],
            ],
            axis=0,
        )
        rows_ref[at * SKEL : (at + 1) * SKEL, :] = both.T.astype(F32)
    pick_rows(lambda at: order_ref[node_order_ref[at]], rows_ref, skel_ref, index_ref, 0, SKEL)
    skel = skel_ref[...].astype(BF).T.astype(F32)
    pt_ref[0] = skel[:features].astype(BF)
    pl.semaphore_wait(barrier, levels + slabs - 1)
    pt_copy(0).start()
    for step in range(1, slabs):
        ask_copy(step).start()

    left_rows_ref[...] = columns_form(skel[:features], width, True).astype(BF).T
    table_ref[...] = kept_table(index_ref[...], count)
    total_ref[...] = skel[features:]

    def zero_dense(at):
        columns = slice(at * SKEL, (at + 1) * SKEL)
        right = columns_form(points_ref[:, columns].astype(F32), width, False).astype(BF)
        dense = dense_of(
            jnp.dot(left_rows_ref[...], right, preferred_element_type=F32), features
        )
        dense_ref[at % 2] = dense
        share_ref[at % 2] = kept_row(table_ref, at * SKEL, SKEL) / jnp.sum(
            dense, axis=0, keepdims=True
        )

    def zero_spread(at):
        total_ref[...] += lax.dot_general(
            weights_ref[:, at * SKEL : (at + 1) * SKEL],
            (dense_ref[at % 2] * share_ref[at % 2]).astype(BF),
            NT,
            preferred_element_type=F32,
        )

    def gather(at):
        for row in range(at * SKEL, (at + 1) * SKEL):
            picked_ref[row : row + 1, :] = rows_ref[order_ref[row]][None]

    def to_tree(at):
        one, begin = at * SKEL // leaf, at * SKEL % leaf
        turn = picked_ref[at * SKEL : (at + 1) * SKEL, :].astype(BF).T
        tree_ref[one, :, begin : begin + SKEL] = turn
        left_ref[one, :, begin : begin + SKEL] = columns_form(
            turn[:features].astype(F32), width, True
        ).astype(BF)

    for at in range(chunks + 1):
        if at < chunks:
            zero_dense(at)
        if at > 0:
            zero_spread(at - 1)
            to_tree(at - 1)
        if at < chunks:
            gather(at)

    wt_ref[0] = total_ref[...].astype(BF)
    wt_copy(0).start()

    def fill(slot_ref, step, table):
        own = lax.broadcasted_iota(jnp.int32, table.shape, 1) == slab
        place = lax.broadcasted_iota(jnp.int32, table.shape, 0)
        for one in range(cap):
            wanted = jnp.max(
                jnp.where(own & (place == one), table, 0).astype(F32), axis=(0, 1), keepdims=True
            )
            slot_ref[step, one] = sum(
                tree_ref[other] * jnp.where(wanted == other, 1.0, 0.0).astype(BF)
                for other in range(leaves)
            )

    for step in reversed(range(1, slabs)):
        ask_copy(step).wait_recv()
        fill(send_ref, step, asked_ref[step])
        near_copy(step).start()

    def merge_points(level):
        upper = bit(level)

        def pair():
            pair_pt[upper] = pt_ref[level]
            pair_pt[1 - upper] = pt_held[level]
            for half in range(2):
                points = pair_pt[half].astype(F32)
                right_ref[half] = columns_form(points, width, False).astype(BF)
                pair_rows[half * SKEL : (half + 1) * SKEL, :] = (
                    columns_form(points, width, True).astype(BF).T.astype(F32)
                )

        def pick(start):
            pick_rows(
                lambda at: merge_ref[level, at], pair_rows, skel_ref, index_ref, start, HALF
            )

        def leave():
            left_rows_ref[...] = skel_ref[...].astype(BF)
            pt_ref[level + 1] = (skel_ref[...] * 0.5).astype(BF).T[:features]
            pt_copy(level + 1).start()
            table_ref[...] = kept_table(index_ref[...], 2 * SKEL)

        def dense(half):
            value = dense_of(
                jnp.dot(left_rows_ref[...], right_ref[half], preferred_element_type=F32), features
            )
            dense_ref[half] = value
            share_ref[half] = kept_row(table_ref, half * SKEL, SKEL) / jnp.sum(
                value, axis=0, keepdims=True
            )

        def spread(half):
            index = index_ref[...]
            for start in range(0, SKEL, LANES):
                columns = slice(start, start + LANES)
                lanes = lax.broadcasted_iota(jnp.int32, index.shape, 1) + (half * SKEL + start)
                spread_ref[half, :, columns] = jnp.where(
                    index == lanes, 1.0, dense_ref[half, :, columns] * share_ref[half, :, columns]
                ).astype(BF)

        return [
            [pair],
            [functools.partial(pick, 0)],
            [functools.partial(pick, HALF)],
            [leave, functools.partial(dense, 0)],
            [functools.partial(spread, 0), functools.partial(dense, 1)],
            [functools.partial(spread, 1)],
        ]

    def beside(parts, turns, tiles):
        for at, part in enumerate(parts):
            share = turns if at == 0 else tile_steps(
                features,
                tiles[len(tiles) * (at - 1) // (len(parts) - 1) : len(tiles) * at // (len(parts) - 1)],
            )

            run(part, share)

    def merge_weights(level):
        upper = bit(level)
        pair_wt[upper] = wt_ref[level]
        pair_wt[1 - upper] = wt_held[level]
        total = sum(
            lax.dot_general(pair_wt[half], spread_ref[half], NT, preferred_element_type=F32)
            for half in range(2)
        )
        wt_ref[level + 1] = total.astype(BF)
        wt_copy(level + 1).start()

    def near_terms(step):
        slots = [near_slot(step, one) for one in range(cap)]
        return sum([slot[0] for slot in slots], []), sum([slot[1] for slot in slots], [])

    def near_slot(step, one):
        target = jnp.maximum(target_ref[one, partner(step)], 0)
        if step == 0:
            origin, place_at = tree_ref, (own_ref[one, slab],)
        else:
            origin, place_at = near_ref, (step, one)

        def turn(start):
            points = origin[(*place_at, slice(0, features), slice(start, start + SKEL))]
            near_right_ref[one, start : start + SKEL, :] = columns_form(
                points.astype(F32), width, False
            ).astype(BF).T

        def tile(begin, start):
            def exponent():
                return jnp.dot(
                    near_right_ref[one, start : start + SKEL, :],
                    left_ref[target, :, begin : begin + TILE],
                    preferred_element_type=F32,
                )

            def use(dense):
                weight = origin[(*place_at, slice(features, width), slice(start, start + SKEL))]
                term = jnp.dot(weight, dense.astype(BF), preferred_element_type=F32)
                place = near_out_ref.at[step, one, :, begin : begin + TILE]
                place[...] = term if start == 0 else place[...] + term

            return exponent, use

        return (
            [functools.partial(turn, start) for start in range(0, leaf, SKEL)],
            [
                tile(begin, start)
                for begin in range(0, leaf, TILE)
                for start in range(0, leaf, SKEL)
            ],
        )

    def far_right(level):
        return columns_form(pt_held[level].astype(F32), width, False).astype(BF).T

    def far_terms(level):
        def turn():
            far_right_ref[...] = far_right(level)

        def tile(one, begin):
            def exponent():
                return jnp.dot(
                    far_right_ref[...],
                    left_ref[one, :, begin : begin + TILE],
                    preferred_element_type=F32,
                )

            def use(dense):
                weight = (wt_held[level].astype(F32) * far_ref[level, 0, one].astype(F32)).astype(BF)
                term = jnp.dot(weight, dense.astype(BF), preferred_element_type=F32)
                place = out_ref.at[one, :, begin : begin + TILE]
                place[...] = term if level == 0 else place[...] + term

            return exponent, use

        return (
            [turn],
            [tile(one, begin) for one in range(leaves) for begin in range(0, leaf, TILE)],
        )

    def alone(terms):
        turns, tiles = terms
        run([*turns, *tile_steps(features, tiles)])

    for level in range(levels - 1):
        pt_copy(level).wait_recv()
        if level == 0:
            beside(merge_points(level), *near_terms(0))
            if slabs > 1:
                near_copy(1).wait_recv()
                alone(near_terms(1))
        else:
            beside(merge_points(level), *far_terms(level - 1))
        wt_copy(level).wait_recv()
        merge_weights(level)
    alone(far_terms(levels - 2))
    for step in reversed(range(2, slabs)):
        near_copy(step).wait_recv()
    pt_copy(levels - 1).wait_recv()
    last_right_ref[...] = far_right(levels - 1)
    wt_copy(levels - 1).wait_recv()
    for one in range(leaves):
        last_weight_ref[one] = (
            wt_held[levels - 1].astype(F32) * far_ref[levels - 1, 0, one].astype(F32)
        ).astype(BF)
    for level in range(levels):
        pt_copy(level).wait_send()
        wt_copy(level).wait_send()
    for step in range(1, slabs):
        ask_copy(step).wait_send()
        near_copy(step).wait_send()


def last_kernel(features, slabs, target_in, far_in, right_ref, weight_ref, left_ref, near_ref,
                far_near_ref, prior_ref, out_in, sum_ref, near_right_ref, target_ref, far_ref,
                input_sem, out_sem):
    loads = [
        pltpu.make_async_copy(target_in, target_ref, input_sem.at[0]),
        pltpu.make_async_copy(far_in, far_ref, input_sem.at[1]),
    ]
    for load in loads:
        load.start()
    leaves, width, leaf = left_ref.shape
    done = near_ref.shape[0]

    def leave(one):
        return pltpu.make_async_copy(
            sum_ref.at[one], out_in.at[:, pl.ds(one * leaf, leaf)], out_sem.at[one]
        )

    def tile(one, begin):
        def exponent():
            return jnp.dot(
                right_ref[...], left_ref[one, :, begin : begin + TILE], preferred_element_type=F32
            )

        def use(dense):
            place = sum_ref.at[one, :, begin : begin + TILE]
            place[...] += jnp.dot(weight_ref[one], dense.astype(BF), preferred_element_type=F32)

        return exponent, use

    def far_leaf(one):
        run(tile_steps(features, [tile(one, begin) for begin in range(0, leaf, TILE)]))

    def near_tile(step, slot, target, begin, start):
        def exponent():
            return jnp.dot(
                near_right_ref[start : start + SKEL, :],
                left_ref[target, :, begin : begin + TILE],
                preferred_element_type=F32,
            )

        def use(dense):
            place = sum_ref.at[target, :, begin : begin + TILE]
            place[...] += jnp.dot(
                far_near_ref[step, slot, features:, start : start + SKEL],
                dense.astype(BF),
                preferred_element_type=F32,
            )

        return exponent, use

    def near_slot(step, slot, target):
        for start in range(0, leaf, SKEL):
            points = far_near_ref[step, slot, :features, start : start + SKEL]
            near_right_ref[start : start + SKEL, :] = columns_form(
                points.astype(F32), width, False
            ).astype(BF).T
        run(tile_steps(features, [
            near_tile(step, slot, target, begin, start)
            for begin in range(0, leaf, TILE)
            for start in range(0, leaf, SKEL)
        ]))

    sum_ref[...] = prior_ref[...]
    far_leaf(0)
    for load in loads:
        load.wait()
    for step in range(slabs):
        owner = partner_of(lax.axis_index("task"), step)
        for slot in range(target_ref.shape[0]):
            target = target_ref[slot, owner]

            @pl.when(target >= 0)
            def _(step=step, slot=slot, target=target):
                if step < done:
                    sum_ref[target] += near_ref[step, slot]
                else:
                    near_slot(step, slot, target)

    leave(0).start()
    for one in range(1, leaves):
        @pl.when(far_ref[far_ref.shape[0] - 1, 0, one] > 0)
        def _(one=one):
            far_leaf(one)

        leave(one).start()
    for one in range(leaves):
        leave(one).wait()


def in_hbm(value):
    return pltpu.with_memory_space_constraint(value, pltpu.HBM)


def body(points, weights, point_order, node_order, merge_order, far_list, task_target, task_source):
    count, features = points.shape
    columns = weights.shape[1]
    width = features + columns
    levels = far_list.shape[3]
    leaves = far_list.shape[2]
    leaf = count // leaves
    slabs, cap = task_source.shape[2:]
    far = far_list.transpose(0, 3, 1, 2)[0]
    source = task_source[0, 0].T
    target = task_target[0, 0].T
    inputs = (points.T, weights.T, point_order[0, 0], node_order[0, 0], merge_order[0, 0], far, source, target)
    total, near, left, right, weight, far_near = pl.pallas_call(
        functools.partial(chain_kernel, features, levels, slabs),
        out_shape=(
            jax.ShapeDtypeStruct((leaves, columns, leaf), F32),
            jax.ShapeDtypeStruct((min(slabs, 2), cap, columns, leaf), F32),
            jax.ShapeDtypeStruct((leaves, width, leaf), BF),
            jax.ShapeDtypeStruct((SKEL, width), BF),
            jax.ShapeDtypeStruct((leaves, columns, SKEL), BF),
            jax.ShapeDtypeStruct((slabs, cap, width, leaf), BF),
        ),
        in_specs=[HBM] * 8,
        out_specs=(VMEM,) * 6,
        scratch_shapes=[
            pltpu.VMEM((features, count), BF),
            pltpu.VMEM((columns, count), BF),
            pltpu.VMEM((count, width), F32),
            pltpu.VMEM((count, width), F32),
            pltpu.VMEM((2, width, SKEL), BF),
            pltpu.VMEM((SKEL, width), F32),
            pltpu.VMEM((SKEL, width), jnp.int32),
            pltpu.VMEM((SKEL, width), BF),
            pltpu.VMEM((LANES, LANES), F32),
            pltpu.VMEM((2, SKEL, SKEL), F32),
            pltpu.VMEM((2, 1, SKEL), F32),
            pltpu.VMEM((columns, SKEL), F32),
            pltpu.VMEM((leaves, width, leaf), BF),
            pltpu.VMEM((levels, features, SKEL), BF),
            pltpu.VMEM((levels, features, SKEL), BF),
            pltpu.VMEM((levels, columns, SKEL), BF),
            pltpu.VMEM((levels, columns, SKEL), BF),
            pltpu.VMEM((2, features, SKEL), BF),
            pltpu.VMEM((2, columns, SKEL), BF),
            pltpu.VMEM((2 * SKEL, width), F32),
            pltpu.VMEM((2, SKEL, SKEL), BF),
            pltpu.VMEM((cap, leaf, width), BF),
            pltpu.VMEM((SKEL, width), BF),
            pltpu.VMEM((slabs, cap, slabs), jnp.int32),
            pltpu.VMEM((slabs, cap, width, leaf), BF),
            pltpu.SMEM((count,), jnp.int32),
            pltpu.SMEM((count,), jnp.int32),
            pltpu.SMEM((levels - 1, 2 * SKEL), jnp.int32),
            pltpu.SMEM(far.shape, jnp.int32),
            pltpu.SMEM(target.shape, jnp.int32),
            pltpu.SMEM(source.shape, jnp.int32),
            pltpu.VMEM(source.shape, jnp.int32),
            pltpu.SemaphoreType.DMA((9,)),
            pltpu.SemaphoreType.DMA((levels,)),
            pltpu.SemaphoreType.DMA((levels,)),
            pltpu.SemaphoreType.DMA((levels,)),
            pltpu.SemaphoreType.DMA((levels,)),
            pltpu.SemaphoreType.DMA((slabs,)),
            pltpu.SemaphoreType.DMA((slabs,)),
            pltpu.SemaphoreType.DMA((slabs,)),
            pltpu.SemaphoreType.DMA((slabs,)),
        ],
        compiler_params=pltpu.CompilerParams(
            collective_id=0, has_side_effects=True, vmem_limit_bytes=48 << 20
        ),
        name="chain",
    )(*[in_hbm(one) for one in inputs])
    out = pl.pallas_call(
        functools.partial(last_kernel, features, slabs),
        out_shape=jax.ShapeDtypeStruct((columns, count), F32),
        in_specs=[HBM] * 2 + [VMEM] * 6,
        out_specs=HBM,
        scratch_shapes=[
            pltpu.VMEM((leaves, columns, leaf), F32),
            pltpu.VMEM((leaf, width), BF),
            pltpu.SMEM(target.shape, jnp.int32),
            pltpu.SMEM(far.shape, jnp.int32),
            pltpu.SemaphoreType.DMA((2,)),
            pltpu.SemaphoreType.DMA((leaves,)),
        ],
        compiler_params=pltpu.CompilerParams(vmem_limit_bytes=48 << 20),
        name="last",
    )(in_hbm(target), in_hbm(far), right, weight, left, near, far_near, total)
    return out.T


def solution(mesh):
    return jax.shard_map(
        body,
        mesh=mesh,
        in_specs=(
            P(("leaf", "task"), None),
            P(("leaf", "task"), None),
            P("leaf", "task", None),
            P("leaf", "task", None),
            P("leaf", "task", None, None),
            P("leaf", "task", None, None),
            P("leaf", "task", None, None),
            P("leaf", "task", None, None),
        ),
        out_specs=P(("leaf", "task"), None),
        check_vma=False,
    )
```

```python
import functools
import math

import jax
import jax.numpy as jnp
from jax import lax
from jax.experimental import pallas as pl
from jax.experimental.pallas import tpu as pltpu
from jax.sharding import PartitionSpec as P

SKEL = 512
KERNEL_SCALE = 1.5
LANES = 128
BF = jnp.bfloat16
F32 = jnp.float32

VMEM = pl.BlockSpec(memory_space=pltpu.VMEM)
HBM = pl.BlockSpec(memory_space=pltpu.HBM)
MESH = pl.DeviceIdType.MESH
NT = (((1,), (1,)), ((), ()))
TILE = 512
HALF = 256


def scale_of(features):
    return KERNEL_SCALE / features * math.log2(math.e)


def pieces(norm):
    first = norm.astype(BF).astype(F32)
    left = norm - first
    second = left.astype(BF).astype(F32)
    third = left - second
    return first, second, third


def columns_form(points, width, left):
    features, count = points.shape
    first, second, third = pieces(jnp.sum(points * points, axis=0, keepdims=True))
    lines = lax.broadcasted_iota(jnp.int32, (8, count), 0)
    at = 0 if left else 3
    ones = 3 - at
    tail = jnp.where((lines >= ones) & (lines < ones + 3), 1.0, 0.0)
    tail = jnp.where(lines == at, -first, tail)
    tail = jnp.where(lines == at + 1, -second, tail)
    tail = jnp.where(lines == at + 2, -third, tail)
    rest = jnp.zeros((width - features - 8, count), F32)
    return jnp.concatenate([points + points if left else points, tail, rest], axis=0)


def dense_of(exponent, features):
    return jnp.exp2(exponent * scale_of(features))


def kept_table(index, count):
    lanes = lax.broadcasted_iota(jnp.int32, index.shape, 1)
    high = jnp.where(lax.shift_right_logical(index, 7) == lanes, 1.0, 0.0).astype(BF).T
    low = jnp.where((index & (LANES - 1)) == lanes, 1.0, 0.0).astype(BF)
    return 1.0 - jnp.dot(high, low, preferred_element_type=F32)


def kept_row(table, start, count):
    rows = [table[at : at + 1, :] for at in range(start // LANES, (start + count) // LANES)]
    return jnp.concatenate(rows, axis=1)


def pick_rows(index_of, rows_ref, skel_ref, index_ref, start, count):
    width = rows_ref.shape[1]
    for at in range(start, start + count):
        index = index_of(at)
        skel_ref[at : at + 1, :] = rows_ref[index][None]
        index_ref[at : at + 1, :] = jnp.full((1, width), index, jnp.int32)


def partner_of(slab, step):
    flips = [1 << at for at in range(step.bit_length()) if step >> at & 1]
    return slab + sum((1 - 2 * (slab // flip % 2)) * flip for flip in flips)


def tile_steps(features, tiles):
    held = []

    def step(tile):
        value = tile[0]() if tile else None
        if held:
            exponent, use = held.pop()
            use(dense_of(exponent, features))
        if tile:
            held.append((value, tile[1]))

    return [functools.partial(step, tile) for tile in [*tiles, None]]


def run(*streams):
    marked = [
        ((at + 0.5) / len(stream), which, step)
        for which, stream in enumerate(streams)
        for at, step in enumerate(stream)
    ]
    for _, _, step in sorted(marked, key=lambda one: one[:2]):
        step()


def chain_kernel(features, levels, slabs, points_in, weights_in, order_in, node_order_in, merge_in,
                 far_in, source_in, target_in,
                 out_ref, near_out_ref, left_ref, last_right_ref, last_weight_ref, near_ref,
                 points_ref, weights_ref, rows_ref, picked_ref, right_ref, skel_ref, index_ref,
                 left_rows_ref, table_ref, dense_ref, share_ref, total_ref, tree_ref, pt_ref, pt_held, wt_ref, wt_held,
                 pair_pt, pair_wt, pair_rows, spread_ref, near_right_ref, far_right_ref,
                 asked_ref, send_ref,
                 order_ref, node_order_ref, merge_ref, far_ref, target_ref, own_ref, source_ref,
                 input_sem, pt_send, pt_recv, wt_send, wt_recv, ask_send, ask_recv, near_send, near_recv):
    loads = [
        pltpu.make_async_copy(source, target, input_sem.at[at])
        for at, (source, target) in enumerate([
            (points_in, points_ref),
            (weights_in, weights_ref),
            (order_in, order_ref),
            (node_order_in, node_order_ref),
            (merge_in, merge_ref),
            (far_in, far_ref),
            (source_in, source_ref),
            (target_in, target_ref),
            (source_in, own_ref),
        ])
    ]
    for load in loads:
        load.start()
    region = lax.axis_index("leaf")
    slab = lax.axis_index("task")
    count = rows_ref.shape[0]
    width = rows_ref.shape[1]
    leaves = left_ref.shape[0]
    leaf = count // leaves
    cap = source_ref.shape[0]
    chunks = count // SKEL

    def bit(level):
        return region // 2**level % 2

    def sibling(level):
        return region + (1 - 2 * bit(level)) * 2**level

    def partner(step):
        return partner_of(slab, step)

    barrier = pltpu.get_barrier_semaphore()
    for level in range(levels):
        pl.semaphore_signal(barrier, inc=1, device_id=(sibling(level), slab), device_id_type=MESH)
    for step in range(1, slabs):
        pl.semaphore_signal(barrier, inc=1, device_id=(region, partner(step)), device_id_type=MESH)

    def to_sibling(level, source, target, send, recv):
        return pltpu.make_async_remote_copy(
            src_ref=source.at[level],
            dst_ref=target.at[level],
            send_sem=send.at[level],
            recv_sem=recv.at[level],
            device_id=(sibling(level), slab),
            device_id_type=MESH,
        )

    def pt_copy(level):
        return to_sibling(level, pt_ref, pt_held, pt_send, pt_recv)

    def wt_copy(level):
        return to_sibling(level, wt_ref, wt_held, wt_send, wt_recv)

    def ask_copy(step):
        return pltpu.make_async_remote_copy(
            src_ref=source_ref,
            dst_ref=asked_ref.at[step],
            send_sem=ask_send.at[step],
            recv_sem=ask_recv.at[step],
            device_id=(region, partner(step)),
            device_id_type=MESH,
        )

    def near_copy(step):
        return pltpu.make_async_remote_copy(
            src_ref=send_ref.at[step],
            dst_ref=near_ref.at[step],
            send_sem=near_send.at[step],
            recv_sem=near_recv.at[step],
            device_id=(region, partner(step)),
            device_id_type=MESH,
        )

    for load in loads:
        load.wait()
    for at in range(chunks):
        both = jnp.concatenate(
            [
                points_ref[:, at * SKEL : (at + 1) * SKEL],
                weights_ref[:, at * SKEL : (at + 1) * SKEL],
            ],
            axis=0,
        )
        rows_ref[at * SKEL : (at + 1) * SKEL, :] = both.T.astype(F32)
    pick_rows(lambda at: order_ref[node_order_ref[at]], rows_ref, skel_ref, index_ref, 0, SKEL)
    skel = skel_ref[...].astype(BF).T.astype(F32)
    pt_ref[0] = skel[:features].astype(BF)
    pl.semaphore_wait(barrier, levels + slabs - 1)
    pt_copy(0).start()
    for step in range(1, slabs):
        ask_copy(step).start()

    left_rows_ref[...] = columns_form(skel[:features], width, True).astype(BF).T
    table_ref[...] = kept_table(index_ref[...], count)
    total_ref[...] = skel[features:]

    def zero_dense(at):
        columns = slice(at * SKEL, (at + 1) * SKEL)
        right = columns_form(points_ref[:, columns].astype(F32), width, False).astype(BF)
        dense = dense_of(
            jnp.dot(left_rows_ref[...], right, preferred_element_type=F32), features
        )
        dense_ref[at % 2] = dense
        share_ref[at % 2] = kept_row(table_ref, at * SKEL, SKEL) / jnp.sum(
            dense, axis=0, keepdims=True
        )

    def zero_spread(at):
        total_ref[...] += lax.dot_general(
            weights_ref[:, at * SKEL : (at + 1) * SKEL],
            (dense_ref[at % 2] * share_ref[at % 2]).astype(BF),
            NT,
            preferred_element_type=F32,
        )

    def gather(at):
        for row in range(at * SKEL, (at + 1) * SKEL):
            picked_ref[row : row + 1, :] = rows_ref[order_ref[row]][None]

    def to_tree(at):
        one, begin = at * SKEL // leaf, at * SKEL % leaf
        turn = picked_ref[at * SKEL : (at + 1) * SKEL, :].astype(BF).T
        tree_ref[one, :, begin : begin + SKEL] = turn
        left_ref[one, :, begin : begin + SKEL] = columns_form(
            turn[:features].astype(F32), width, True
        ).astype(BF)

    for at in range(chunks + 1):
        if at < chunks:
            zero_dense(at)
        if at > 0:
            zero_spread(at - 1)
            to_tree(at - 1)
        if at < chunks:
            gather(at)

    wt_ref[0] = total_ref[...].astype(BF)
    wt_copy(0).start()

    def fill(slot_ref, step, table):
        own = lax.broadcasted_iota(jnp.int32, table.shape, 1) == slab
        place = lax.broadcasted_iota(jnp.int32, table.shape, 0)
        for one in range(cap):
            wanted = jnp.max(
                jnp.where(own & (place == one), table, 0).astype(F32), axis=(0, 1), keepdims=True
            )
            slot_ref[step, one] = sum(
                tree_ref[other] * jnp.where(wanted == other, 1.0, 0.0).astype(BF)
                for other in range(leaves)
            )

    for step in reversed(range(1, slabs)):
        ask_copy(step).wait_recv()
        fill(send_ref, step, asked_ref[step])
        near_copy(step).start()

    def merge_points(level):
        upper = bit(level)

        def pair():
            pair_pt[upper] = pt_ref[level]
            pair_pt[1 - upper] = pt_held[level]
            for half in range(2):
                points = pair_pt[half].astype(F32)
                right_ref[half] = columns_form(points, width, False).astype(BF)
                pair_rows[half * SKEL : (half + 1) * SKEL, :] = (
                    columns_form(points, width, True).astype(BF).T.astype(F32)
                )

        def pick(start):
            pick_rows(
                lambda at: merge_ref[level, at], pair_rows, skel_ref, index_ref, start, HALF
            )

        def leave():
            left_rows_ref[...] = skel_ref[...].astype(BF)
            pt_ref[level + 1] = (skel_ref[...] * 0.5).astype(BF).T[:features]
            pt_copy(level + 1).start()
            table_ref[...] = kept_table(index_ref[...], 2 * SKEL)

        def dense(half):
            value = dense_of(
                jnp.dot(left_rows_ref[...], right_ref[half], preferred_element_type=F32), features
            )
            dense_ref[half] = value
            share_ref[half] = kept_row(table_ref, half * SKEL, SKEL) / jnp.sum(
                value, axis=0, keepdims=True
            )

        def spread(half):
            index = index_ref[...]
            for start in range(0, SKEL, LANES):
                columns = slice(start, start + LANES)
                lanes = lax.broadcasted_iota(jnp.int32, index.shape, 1) + (half * SKEL + start)
                spread_ref[half, :, columns] = jnp.where(
                    index == lanes, 1.0, dense_ref[half, :, columns] * share_ref[half, :, columns]
                ).astype(BF)

        return [
            [pair],
            [functools.partial(pick, 0)],
            [functools.partial(pick, HALF)],
            [leave, functools.partial(dense, 0)],
            [functools.partial(spread, 0), functools.partial(dense, 1)],
            [functools.partial(spread, 1)],
        ]

    def beside(parts, turns, tiles):
        for at, part in enumerate(parts):
            share = turns if at == 0 else tile_steps(
                features,
                tiles[len(tiles) * (at - 1) // (len(parts) - 1) : len(tiles) * at // (len(parts) - 1)],
            )

            run(part, share)

    def merge_weights(level):
        upper = bit(level)
        pair_wt[upper] = wt_ref[level]
        pair_wt[1 - upper] = wt_held[level]
        total = sum(
            lax.dot_general(pair_wt[half], spread_ref[half], NT, preferred_element_type=F32)
            for half in range(2)
        )
        wt_ref[level + 1] = total.astype(BF)
        wt_copy(level + 1).start()

    def near_terms(step):
        slots = [near_slot(step, one) for one in range(cap)]
        return sum([slot[0] for slot in slots], []), sum([slot[1] for slot in slots], [])

    def near_slot(step, one):
        target = jnp.maximum(target_ref[one, partner(step)], 0)
        if step == 0:
            origin, place_at = tree_ref, (own_ref[one, slab],)
        else:
            origin, place_at = near_ref, (step, one)

        def turn(start):
            points = origin[(*place_at, slice(0, features), slice(start, start + SKEL))]
            near_right_ref[one, start : start + SKEL, :] = columns_form(
                points.astype(F32), width, False
            ).astype(BF).T

        def tile(begin, start):
            def exponent():
                return jnp.dot(
                    near_right_ref[one, start : start + SKEL, :],
                    left_ref[target, :, begin : begin + TILE],
                    preferred_element_type=F32,
                )

            def use(dense):
                weight = origin[(*place_at, slice(features, width), slice(start, start + SKEL))]
                term = jnp.dot(weight, dense.astype(BF), preferred_element_type=F32)
                place = near_out_ref.at[step, one, :, begin : begin + TILE]
                place[...] = term if start == 0 else place[...] + term

            return exponent, use

        return (
            [functools.partial(turn, start) for start in range(0, leaf, SKEL)],
            [
                tile(begin, start)
                for begin in range(0, leaf, TILE)
                for start in range(0, leaf, SKEL)
            ],
        )

    def far_right(level):
        return columns_form(pt_held[level].astype(F32), width, False).astype(BF).T

    def far_terms(level):
        def turn():
            far_right_ref[...] = far_right(level)

        def tile(one, begin):
            def exponent():
                return jnp.dot(
                    far_right_ref[...],
                    left_ref[one, :, begin : begin + TILE],
                    preferred_element_type=F32,
                )

            def use(dense):
                weight = (wt_held[level].astype(F32) * far_ref[level, 0, one].astype(F32)).astype(BF)
                term = jnp.dot(weight, dense.astype(BF), preferred_element_type=F32)
                place = out_ref.at[one, :, begin : begin + TILE]
                place[...] = term if level == 0 else place[...] + term

            return exponent, use

        return (
            [turn],
            [tile(one, begin) for one in range(leaves) for begin in range(0, leaf, TILE)],
        )

    def alone(terms):
        turns, tiles = terms
        run([*turns, *tile_steps(features, tiles)])

    for level in range(levels - 1):
        pt_copy(level).wait_recv()
        if level < min(slabs, 2):
            if level > 0:
                near_copy(level).wait_recv()
            beside(merge_points(level), *near_terms(level))
        else:
            beside(merge_points(level), [], [])
        wt_copy(level).wait_recv()
        merge_weights(level)
    for level in range(levels - 1):
        alone(far_terms(level))
    for step in reversed(range(2, slabs)):
        near_copy(step).wait_recv()
    pt_copy(levels - 1).wait_recv()
    last_right_ref[...] = far_right(levels - 1)
    wt_copy(levels - 1).wait_recv()
    for one in range(leaves):
        last_weight_ref[one] = (
            wt_held[levels - 1].astype(F32) * far_ref[levels - 1, 0, one].astype(F32)
        ).astype(BF)
    for level in range(levels):
        pt_copy(level).wait_send()
        wt_copy(level).wait_send()
    for step in range(1, slabs):
        ask_copy(step).wait_send()
        near_copy(step).wait_send()


def last_kernel(features, slabs, target_in, far_in, right_ref, weight_ref, left_ref, near_ref,
                far_near_ref, prior_ref, out_in, sum_ref, near_right_ref, target_ref, far_ref,
                input_sem, out_sem):
    loads = [
        pltpu.make_async_copy(target_in, target_ref, input_sem.at[0]),
        pltpu.make_async_copy(far_in, far_ref, input_sem.at[1]),
    ]
    for load in loads:
        load.start()
    leaves, width, leaf = left_ref.shape
    done = near_ref.shape[0]

    def leave(one):
        return pltpu.make_async_copy(
            sum_ref.at[one], out_in.at[:, pl.ds(one * leaf, leaf)], out_sem.at[one]
        )

    def tile(one, begin):
        def exponent():
            return jnp.dot(
                right_ref[...], left_ref[one, :, begin : begin + TILE], preferred_element_type=F32
            )

        def use(dense):
            place = sum_ref.at[one, :, begin : begin + TILE]
            place[...] += jnp.dot(weight_ref[one], dense.astype(BF), preferred_element_type=F32)

        return exponent, use

    def far_leaf(one):
        run(tile_steps(features, [tile(one, begin) for begin in range(0, leaf, TILE)]))

    def near_tile(step, slot, target, begin, start):
        def exponent():
            return jnp.dot(
                near_right_ref[start : start + SKEL, :],
                left_ref[target, :, begin : begin + TILE],
                preferred_element_type=F32,
            )

        def use(dense):
            place = sum_ref.at[target, :, begin : begin + TILE]
            place[...] += jnp.dot(
                far_near_ref[step, slot, features:, start : start + SKEL],
                dense.astype(BF),
                preferred_element_type=F32,
            )

        return exponent, use

    def near_slot(step, slot, target):
        for start in range(0, leaf, SKEL):
            points = far_near_ref[step, slot, :features, start : start + SKEL]
            near_right_ref[start : start + SKEL, :] = columns_form(
                points.astype(F32), width, False
            ).astype(BF).T
        run(tile_steps(features, [
            near_tile(step, slot, target, begin, start)
            for begin in range(0, leaf, TILE)
            for start in range(0, leaf, SKEL)
        ]))

    sum_ref[...] = prior_ref[...]
    far_leaf(0)
    for load in loads:
        load.wait()
    for step in range(slabs):
        owner = partner_of(lax.axis_index("task"), step)
        for slot in range(target_ref.shape[0]):
            target = target_ref[slot, owner]

            @pl.when(target >= 0)
            def _(step=step, slot=slot, target=target):
                if step < done:
                    sum_ref[target] += near_ref[step, slot]
                else:
                    near_slot(step, slot, target)

    leave(0).start()
    for one in range(1, leaves):
        @pl.when(far_ref[far_ref.shape[0] - 1, 0, one] > 0)
        def _(one=one):
            far_leaf(one)

        leave(one).start()
    for one in range(leaves):
        leave(one).wait()


def in_hbm(value):
    return pltpu.with_memory_space_constraint(value, pltpu.HBM)


def body(points, weights, point_order, node_order, merge_order, far_list, task_target, task_source):
    count, features = points.shape
    columns = weights.shape[1]
    width = features + columns
    levels = far_list.shape[3]
    leaves = far_list.shape[2]
    leaf = count // leaves
    slabs, cap = task_source.shape[2:]
    far = far_list.transpose(0, 3, 1, 2)[0]
    source = task_source[0, 0].T
    target = task_target[0, 0].T
    inputs = (points.T, weights.T, point_order[0, 0], node_order[0, 0], merge_order[0, 0], far, source, target)
    total, near, left, right, weight, far_near = pl.pallas_call(
        functools.partial(chain_kernel, features, levels, slabs),
        out_shape=(
            jax.ShapeDtypeStruct((leaves, columns, leaf), F32),
            jax.ShapeDtypeStruct((min(slabs, 2), cap, columns, leaf), F32),
            jax.ShapeDtypeStruct((leaves, width, leaf), BF),
            jax.ShapeDtypeStruct((SKEL, width), BF),
            jax.ShapeDtypeStruct((leaves, columns, SKEL), BF),
            jax.ShapeDtypeStruct((slabs, cap, width, leaf), BF),
        ),
        in_specs=[HBM] * 8,
        out_specs=(VMEM,) * 6,
        scratch_shapes=[
            pltpu.VMEM((features, count), BF),
            pltpu.VMEM((columns, count), BF),
            pltpu.VMEM((count, width), F32),
            pltpu.VMEM((count, width), F32),
            pltpu.VMEM((2, width, SKEL), BF),
            pltpu.VMEM((SKEL, width), F32),
            pltpu.VMEM((SKEL, width), jnp.int32),
            pltpu.VMEM((SKEL, width), BF),
            pltpu.VMEM((LANES, LANES), F32),
            pltpu.VMEM((2, SKEL, SKEL), F32),
            pltpu.VMEM((2, 1, SKEL), F32),
            pltpu.VMEM((columns, SKEL), F32),
            pltpu.VMEM((leaves, width, leaf), BF),
            pltpu.VMEM((levels, features, SKEL), BF),
            pltpu.VMEM((levels, features, SKEL), BF),
            pltpu.VMEM((levels, columns, SKEL), BF),
            pltpu.VMEM((levels, columns, SKEL), BF),
            pltpu.VMEM((2, features, SKEL), BF),
            pltpu.VMEM((2, columns, SKEL), BF),
            pltpu.VMEM((2 * SKEL, width), F32),
            pltpu.VMEM((2, SKEL, SKEL), BF),
            pltpu.VMEM((cap, leaf, width), BF),
            pltpu.VMEM((SKEL, width), BF),
            pltpu.VMEM((slabs, cap, slabs), jnp.int32),
            pltpu.VMEM((slabs, cap, width, leaf), BF),
            pltpu.SMEM((count,), jnp.int32),
            pltpu.SMEM((count,), jnp.int32),
            pltpu.SMEM((levels - 1, 2 * SKEL), jnp.int32),
            pltpu.SMEM(far.shape, jnp.int32),
            pltpu.SMEM(target.shape, jnp.int32),
            pltpu.SMEM(source.shape, jnp.int32),
            pltpu.VMEM(source.shape, jnp.int32),
            pltpu.SemaphoreType.DMA((9,)),
            pltpu.SemaphoreType.DMA((levels,)),
            pltpu.SemaphoreType.DMA((levels,)),
            pltpu.SemaphoreType.DMA((levels,)),
            pltpu.SemaphoreType.DMA((levels,)),
            pltpu.SemaphoreType.DMA((slabs,)),
            pltpu.SemaphoreType.DMA((slabs,)),
            pltpu.SemaphoreType.DMA((slabs,)),
            pltpu.SemaphoreType.DMA((slabs,)),
        ],
        compiler_params=pltpu.CompilerParams(
            collective_id=0, has_side_effects=True, vmem_limit_bytes=48 << 20
        ),
        name="chain",
    )(*[in_hbm(one) for one in inputs])
    out = pl.pallas_call(
        functools.partial(last_kernel, features, slabs),
        out_shape=jax.ShapeDtypeStruct((columns, count), F32),
        in_specs=[HBM] * 2 + [VMEM] * 6,
        out_specs=HBM,
        scratch_shapes=[
            pltpu.VMEM((leaves, columns, leaf), F32),
            pltpu.VMEM((leaf, width), BF),
            pltpu.SMEM(target.shape, jnp.int32),
            pltpu.SMEM(far.shape, jnp.int32),
            pltpu.SemaphoreType.DMA((2,)),
            pltpu.SemaphoreType.DMA((leaves,)),
        ],
        compiler_params=pltpu.CompilerParams(vmem_limit_bytes=48 << 20),
        name="last",
    )(in_hbm(target), in_hbm(far), right, weight, left, near, far_near, total)
    return out.T


def solution(mesh):
    return jax.shard_map(
        body,
        mesh=mesh,
        in_specs=(
            P(("leaf", "task"), None),
            P(("leaf", "task"), None),
            P("leaf", "task", None),
            P("leaf", "task", None),
            P("leaf", "task", None, None),
            P("leaf", "task", None, None),
            P("leaf", "task", None, None),
            P("leaf", "task", None, None),
        ),
        out_specs=P(("leaf", "task"), None),
        check_vma=False,
    )
```
